32 devices in a mesh: space: 4 (over z), vel: 8 (over y, x, core).
Axes of the slice: x: 2, y: 2, z: 4, core: 2. Of those that a mesh axis runs over, the one named last changes fastest.
Arguments:
- dist: float32 [64, 16, 16, 2048], P('space', None, None, 'vel'), may hold values from 0.05 to 2
- relax_rate: float32 [64, 16, 16], P('space'), may hold values from 0.2 to 0.9
- kinetic_cells: int32 [2, 16384], P(None, 'space'), may hold values from 0 to 4095, as said below
- kinetic_count: int32 [2, 4], replicated, may hold values from 1 to 4096, 8192 in all within a row
- map_a: bfloat16 [2048, 768], replicated, may hold values from -0.125 to 0.125
- map_b: bfloat16 [2048, 768], replicated, may hold values from -0.125 to 0.125
- map_c: bfloat16 [768, 2048], replicated, may hold values from -0.21875 to 0.21875
Outputs:
- dist_out: float32 [64, 16, 16, 2048], P('space', None, None, 'vel')
The draws below stay inside these ranges and needn't reach their ends.
Inputs may be any that keep to these rules, and one draw needn't show every extreme that they name: `kinetic_cells`: for each step, the 4096 entries of a slab's block are a permutation of that slab's local cell numbers. `kinetic_count`: each step's counts sum to 8192, and one slab is kinetic in all its cells.
All inputs are finite; a program needn't handle non-finite values.
Results may differ from the reference program's by a relative error of at most 0.0034.
Values may be sent and summed in bfloat16 or wider, within the bound.
A program may use at most 128 MiB of HBM per device.

```python
import math
import jax
import jax.numpy as jnp
import numpy as np
from jax import lax

GX = 16
GY = 16
GZ = 8
RANK = 768
STEPS = 2
CX = 16
NY = 16
NZ = 16
NV = 2048
NX = 64
KMEAN = 2048
KTOT = 8192
N_SPACE = 4
N_VEL = 8


def draw_kinetic_cells(key, part):
    block_keys = jax.random.split(jax.random.fold_in(key, 17), STEPS * N_SPACE)
    chosen = jax.vmap(lambda one_key: jax.random.permutation(one_key, CX * NY * NZ))(block_keys)
    return chosen.reshape(STEPS, N_SPACE * CX * NY * NZ).astype(jnp.int32)


def levels(key, dims, cuts, least, top_value):
    def one(dim, blocks):
        heights = jax.random.uniform(jax.random.fold_in(jax.random.fold_in(key, 6), dim), (blocks,), jnp.float32, least / len(cuts), top_value / len(cuts))
        return jnp.repeat(jnp.exp(heights), dims[dim] // blocks).reshape((-1,) + (1,) * (len(dims) - dim - 1))

    factor_of = one(*cuts[0])
    for cut in cuts[1:]:
        factor_of = factor_of * one(*cut)
    return factor_of


def profile(number_of, total, most, lean):
    loads = [(1 << 20) // math.isqrt(grade ** lean) + 1 for grade in range(2, number_of + 1)]
    spare, given = total - most - (number_of - 1), [1] * (number_of - 1)
    while spare > 0:
        free = [i for i in range(number_of - 1) if given[i] < most]
        pool, left = sum([loads[i] for i in free]), spare
        for i in free:
            more = min(most - given[i], max(1, left * loads[i] // pool), spare)
            given[i] = given[i] + more
            spare = spare - more
    return np.array([most] + given)


def uneven(rng, number_of, total, bound, slope):
    if number_of == 2:
        one = jax.random.randint(rng, (), max(1, total - bound), min(bound, total - 1) + 1)
        return jnp.stack([one, total - one])
    sizes = jnp.asarray(profile(number_of, total, bound, slope), jnp.int32)
    pairs = (number_of - 1) // 2
    donor, sink = sizes[1:1 + 2 * pairs:2], sizes[2:2 + 2 * pairs:2]
    slack = jnp.minimum(donor - 1, bound - sink)
    moved = jax.random.randint(jax.random.fold_in(rng, 1), (pairs,), 0, 1 << 20) % (slack + 1)
    sizes = sizes.at[1:1 + 2 * pairs:2].set(donor - moved).at[2:2 + 2 * pairs:2].set(sink + moved)
    return sizes[jax.random.permutation(jax.random.fold_in(rng, 2), number_of)]


def centred(key, dims, scale, limit, held_as=jnp.bfloat16):
    result = jax.random.normal(key, dims, jnp.float32) * scale
    return jnp.minimum(jnp.maximum(result, -limit), limit).astype(held_as)


def setup_inputs(seed: int = 0) -> dict:
    key_list = jax.random.split(jax.random.key(seed), 8)
    dist = jnp.clip(jnp.exp(math.log(2.0) - 3.6888794 * jax.random.uniform(key_list[0], (NX, NY, NZ, NV), jnp.float32) ** levels(key_list[0], (NX, NY, NZ, NV), ((0, 4), (3, 8)), -0.2, 0.2)), 0.05, 2.0)
    relax_rate = jnp.clip(0.2 + 0.7 * jax.random.uniform(key_list[1], (NX, NY, NZ), jnp.float32) ** levels(key_list[1], (NX, NY, NZ), ((0, 4),), -0.2, 0.2), 0.2, 0.9)
    kinetic_cells = draw_kinetic_cells(jax.random.fold_in(key_list[7], 71), 0)
    kinetic_count = jax.vmap(lambda own: uneven(own, N_SPACE, KTOT, CX * NY * NZ, 2))(jax.random.split(key_list[3], STEPS)).reshape((STEPS, N_SPACE)).astype(jnp.int32)
    map_a = centred(key_list[4], (NV, RANK), NV ** -0.5, 0.125)
    map_b = centred(key_list[5], (NV, RANK), NV ** -0.5, 0.125)
    map_c = centred(key_list[6], (RANK, NV), RANK ** -0.5, 0.21875)
    return dict(dist=dist, relax_rate=relax_rate, kinetic_cells=kinetic_cells, kinetic_count=kinetic_count, map_a=map_a, map_b=map_b, map_c=map_c)


COURANT = 0.1
SPACING = 0.5
COLLIDE = 0.5


def velocity_tables():
    grid_index = jnp.arange(GX * GY * GZ, dtype=jnp.int32)
    along_x = ((grid_index // (GY * GZ)).astype(jnp.float32) - 0.5 * (GX - 1)) * SPACING
    along_y = (((grid_index // GZ) % GY).astype(jnp.float32) - 0.5 * (GY - 1)) * SPACING
    along_z = ((grid_index % GZ).astype(jnp.float32) - 0.5 * (GZ - 1)) * SPACING
    speed_sq = along_x * along_x + along_y * along_y + along_z * along_z
    weights = jnp.exp(-0.5 * speed_sq)
    weights = weights / jnp.sum(weights)
    moment_basis = jnp.stack([jnp.ones_like(along_x), along_x, along_y, along_z, speed_sq])
    consts = (jnp.sum(weights * along_x * along_x), jnp.sum(weights * along_y * along_y),
              jnp.sum(weights * along_z * along_z), jnp.sum(weights * speed_sq),
              jnp.sum(weights * speed_sq * speed_sq))
    return moment_basis, moment_basis * weights[None, :], consts


def coefficients(moments, consts):
    thermal = (moments[4] - consts[3] * moments[0]) / (consts[4] - consts[3] * consts[3])
    return jnp.stack([moments[0] - consts[3] * thermal, moments[1] / consts[0],
                      moments[2] / consts[1], moments[3] / consts[2], thermal])


def limited_slope(first_diff, second_diff):
    return 0.5 * (jnp.sign(first_diff) + jnp.sign(second_diff)) * jnp.minimum(jnp.abs(first_diff), jnp.abs(second_diff))


def face_flux(padded, velocity, direction):
    extent = padded.shape[direction] - 4
    def window(array, offset, amount):
        return lax.slice_in_dim(array, offset, offset + amount, axis=direction)
    diffs = window(padded, 1, extent + 3) - window(padded, 0, extent + 3)
    left_state = window(padded, 1, extent + 1) + 0.5 * limited_slope(window(diffs, 0, extent + 1), window(diffs, 1, extent + 1))
    right_state = window(padded, 2, extent + 1) - 0.5 * limited_slope(window(diffs, 1, extent + 1), window(diffs, 2, extent + 1))
    fluxes = jnp.maximum(velocity, 0.0) * left_state + jnp.minimum(velocity, 0.0) * right_state
    return window(fluxes, 1, extent) - window(fluxes, 0, extent)


def periodic_pad(current, direction):
    extent = current.shape[direction]
    return jnp.concatenate([lax.slice_in_dim(current, extent - 2, extent, axis=direction), current,
                            lax.slice_in_dim(current, 0, 2, axis=direction)], axis=direction)


def transport(padded, current, speed_x, speed_y, speed_z):
    change = face_flux(padded, speed_x, 0) + face_flux(periodic_pad(current, 1), speed_y, 1)
    change = change + face_flux(periodic_pad(current, 2), speed_z, 2)
    return current - COURANT * change


def collide(row_block, map_a, map_b, map_c):
    first_map = jnp.dot(row_block, map_a, preferred_element_type=jnp.float32)
    second_map = jnp.dot(row_block, map_b, preferred_element_type=jnp.float32)
    hidden = (first_map * second_map).astype(jnp.bfloat16)
    return jnp.dot(hidden, map_c, preferred_element_type=jnp.float32).astype(jnp.bfloat16)


def reference(dist, relax_rate, kinetic_cells, kinetic_count, map_a, map_b, map_c):
    vel_width = NV // N_VEL
    moment_basis, weighted, consts = velocity_tables()
    cell_total = NX * NY * NZ
    slab_cells = cell_total // N_SPACE
    current = jnp.moveaxis(dist.reshape(NX, NY, NZ, N_VEL, vel_width), 3, 0)
    speeds = moment_basis[1:4].reshape(3, N_VEL, vel_width)
    grouped_basis = moment_basis.reshape(5, N_VEL, vel_width)
    grouped_weighted = weighted.reshape(5, N_VEL, vel_width)
    relax_rows = relax_rate.reshape(1, cell_total, 1)
    for step_index in range(STEPS):
        advected = lax.map(lambda member: transport(periodic_pad(member[0], 0), member[0], member[1], member[2], member[3]),
                           (current, speeds[0], speeds[1], speeds[2]))
        flat_rows = advected.reshape(N_VEL, cell_total, vel_width)
        moments = jnp.einsum("mgv,gcv->mc", grouped_basis, flat_rows, precision=lax.Precision.HIGHEST)
        coeffs = coefficients(moments, consts)
        equilibrium = jnp.einsum("mc,mgv->gcv", coeffs, grouped_weighted, precision=lax.Precision.HIGHEST)
        relaxed = flat_rows + relax_rows * (equilibrium - flat_rows)
        slab_counts = kinetic_count[step_index].astype(jnp.int32)
        slab_ends = jnp.cumsum(slab_counts).astype(jnp.int32)
        slab_starts = slab_ends - slab_counts
        global_slot = jnp.arange(KTOT, dtype=jnp.int32)
        owner_slab = jnp.sum((slab_ends[None, :] <= global_slot[:, None]).astype(jnp.int32), axis=1).astype(jnp.int32)
        position = global_slot - slab_starts[owner_slab]
        local_cell = kinetic_cells[step_index][owner_slab * slab_cells + position]
        global_rows = (owner_slab * slab_cells + local_cell).astype(jnp.int32)
        kin_rows = jnp.moveaxis(flat_rows[:, global_rows, :], 0, 1).reshape(KTOT, NV)
        collided = lax.map(lambda row_block: collide(row_block, map_a, map_b, map_c),
                           kin_rows.astype(jnp.bfloat16).reshape(KTOT // KMEAN, KMEAN, NV)).reshape(KTOT, NV)
        kinetic = kin_rows + COLLIDE * collided.astype(jnp.float32)
        kinetic_grouped = jnp.moveaxis(kinetic.reshape(KTOT, N_VEL, vel_width), 1, 0)
        updated = relaxed.at[:, global_rows, :].set(kinetic_grouped)
        current = updated.reshape(N_VEL, NX, NY, NZ, vel_width)
    return jnp.moveaxis(current, 0, 3).reshape(NX, NY, NZ, NV)
```

```python
import functools

import jax
import jax.numpy as jnp
import numpy as np
from jax import lax
from jax.experimental import pallas as pl
from jax.experimental.pallas import tpu as pltpu
from jax.sharding import PartitionSpec as P

GX = 16
GY = 16
GZ = 8
STEPS = 2
COURANT = 0.1
SPACING = 0.5
COLLIDE = 0.5
LANES = 128
TILE = 256
HALVES = 2
MESH = pl.DeviceIdType.MESH


def tables():
    k = np.arange(GX * GY * GZ)
    vx = ((k // (GY * GZ)) - 0.5 * (GX - 1)) * SPACING
    vy = (((k // GZ) % GY) - 0.5 * (GY - 1)) * SPACING
    vz = ((k % GZ) - 0.5 * (GZ - 1)) * SPACING
    s = vx * vx + vy * vy + vz * vz
    w = np.exp(-0.5 * s)
    w = w / w.sum()
    m2, m4 = (w * s).sum(), (w * s * s).sum()
    kappa = m4 - m2 * m2
    per_e = w * (s - m2) / kappa
    rows = np.stack([
        w - m2 * per_e,
        w * vx / (w * vx * vx).sum(),
        w * vy / (w * vy * vy).sum(),
        w * vz / (w * vz * vz).sum(),
        per_e,
        per_e,
    ])
    s_hi = np.asarray(np.asarray(s, np.float32).astype(jnp.bfloat16), np.float64)
    cols = np.stack([np.ones_like(vx), vx, vy, vz, s_hi, s - s_hi], axis=1)
    g_hi = np.asarray(np.asarray(rows, np.float32).astype(jnp.bfloat16), np.float64)
    g_lo = rows - g_hi
    basis = np.zeros((k.size, LANES))
    back = np.zeros((LANES, k.size))
    for at, part in ((0, g_hi), (8, g_hi), (16, g_lo)):
        basis[:, at:at + 6] = cols
        back[at:at + 6] = part
    return basis.astype(np.float32).astype(jnp.bfloat16), back.astype(np.float32).astype(jnp.bfloat16)


def limited(a, b):
    return jnp.minimum(jnp.maximum(a, jnp.minimum(b, 0.0)), jnp.maximum(b, 0.0))


def state(up, mid, down):
    return mid + 0.5 * limited(mid - up, down - mid)


def kernel(dims, counts, kin_cells, relax, dist, a_hbm, b_hbm, c_hbm, basis_hbm, back_hbm,
           ret_out,
           cur, cprev, sendbuf, zsend, zrecv, recv, fown, fsend, halo, mv, outbuf,
           map_a, map_b, map_c, basis, hid, coef,
           load_sem, const_sem, local_sem, z_send, z_recv, row_send, row_recv, halo_send, halo_recv, res_send, res_recv):
    nx, ny, nz, width, groups, slabs = dims
    plane = ny * nz
    cells = nx * plane
    nv = groups * width
    rank = map_a.shape[1]
    ppd = nx // groups
    hy = ny // HALVES
    half = hy * nz
    block_rows = ppd * half
    tiles = width // LANES
    nchips = groups // 2
    ncol = groups // 4
    me = lax.axis_index("vel")
    slab = lax.axis_index("space")
    first_x = lax.div(me * width, GY * GZ)
    bit = lax.div(first_x, GX // 2)
    sign = 2 * bit - 1
    ahead = lax.rem(slab + sign + slabs, slabs)
    behind = lax.rem(slab - sign + slabs, slabs)

    def vel_of(s, p):
        q = lax.rem(lax.div(p, 2) + nchips * slabs - s, nchips)
        y = lax.div(q, ncol)
        x = lax.rem(q, ncol)
        return (y * ncol + x + y * (ncol - 1 - 2 * x)) * 2 + lax.rem(p, 2)

    def chain_of(s, v):
        chip = lax.div(v, 2)
        y = lax.div(chip, ncol)
        x = lax.rem(chip, ncol)
        q = y * ncol + x + y * (ncol - 1 - 2 * x)
        return 2 * lax.rem(q + s, nchips) + lax.rem(v, 2)

    mine = chain_of(slab, me)

    def along(r):
        at = mine + r + groups
        s = lax.rem(slab + lax.div(at, groups) - 1 + slabs, slabs)
        return {"space": s, "vel": vel_of(s, lax.rem(at, groups))}

    pieces = 4
    loads = []
    for c in range(pieces):
        size = cells // pieces
        loads.append(pltpu.make_async_copy(
            dist.at[pl.ds(c * size, size)], cur.at[pl.ds(2 * plane + c * size, size)], load_sem.at[c]))
        loads[-1].start()
    consts = []
    for n, (src, dst) in enumerate(((a_hbm, map_a), (b_hbm, map_b), (c_hbm, map_c.at[pl.ds(0, rank)]),
                                    (back_hbm, map_c.at[pl.ds(rank, LANES)]), (basis_hbm, basis))):
        consts.append(pltpu.make_async_copy(src, dst, const_sem.at[n]))
        consts[-1].start()

    reach = 1 if ppd > 1 else 2
    barrier = pltpu.get_barrier_semaphore()
    for p in range(1, groups):
        pl.semaphore_signal(barrier, inc=1, device_id={"vel": lax.rem(me + p, groups)}, device_id_type=MESH)
    pl.semaphore_signal(barrier, inc=1, device_id={"space": ahead}, device_id_type=MESH)
    pl.semaphore_signal(barrier, inc=1, device_id={"space": behind}, device_id_type=MESH)
    for r in range(1, reach + 1):
        pl.semaphore_signal(barrier, inc=1, device_id=along(r), device_id_type=MESH)
        pl.semaphore_signal(barrier, inc=1, device_id=along(-r), device_id_type=MESH)
    pl.semaphore_wait(barrier, groups + 1 + 2 * reach)

    lane = lax.broadcasted_iota(jnp.int32, (1, LANES), 1)
    vy = (((lane // GZ) % GY).astype(jnp.float32) - 0.5 * (GY - 1)) * SPACING
    vz = ((lane % GZ).astype(jnp.float32) - 0.5 * (GZ - 1)) * SPACING
    block = (nz, LANES)
    pos_y = jnp.broadcast_to(vy > 0.0, block)
    pos_z = jnp.broadcast_to(vz > 0.0, block)
    half_y = jnp.broadcast_to(jnp.where(vy > 0.0, 0.5, -0.5), block)
    half_z = jnp.broadcast_to(jnp.where(vz > 0.0, 0.5, -0.5), block)
    rate_y = jnp.broadcast_to(COURANT * jnp.abs(vy), block)
    rate_z = jnp.broadcast_to(COURANT * jnp.abs(vz), block)

    def pick(positive, negative):
        return bit * positive + (1 - bit) * negative

    def across(value, emit):
        def y_state(mid, before, after):
            return mid + half_y * limited(before, after)

        f = {y: value(y) for y in range(-2, 2)}
        d = {y: f[y + 1] - f[y] for y in (-2, -1, 0)}
        cy = {y: y_state(f[y], d[y - 1], d[y]) for y in (-1, 0)}
        for y in range(hy):
            f[y + 2] = value(y + 2)
            d[y + 1] = f[y + 2] - f[y + 1]
            cy[y + 1] = y_state(f[y + 1], d[y], d[y + 1])
            mid = f[y]
            total = rate_y * (cy[y] - jnp.where(pos_y, cy[y - 1], cy[y + 1]))
            dz = pltpu.roll(mid, nz - 1, 0) - mid
            cz = mid + half_z * limited(pltpu.roll(dz, 1, 0), dz)
            total += rate_z * (cz - jnp.where(pos_z, pltpu.roll(cz, 1, 0), pltpu.roll(cz, nz - 1, 0)))
            emit(y, mid, total)

    def speed(tile):
        return COURANT * jnp.abs((tile.astype(jnp.float32) - 0.5 * (GX - 1)) * SPACING)

    def transport(dest, h):
        def row(y):
            return lax.rem(h * hy + y + ny, ny) * nz

        @pl.loop(0, tiles)
        def _(t):
            cols = pl.ds(pl.multiple_of(t * LANES, LANES), LANES)
            rate_x = speed(lax.div(me * width + t * LANES, GY * GZ))
            for j in range(ppd):
                index = 2 + dest * ppd + pick(j, ppd - 1 - j)

                def at(k, y):
                    return cur[pl.ds(pl.multiple_of(k * plane + row(y), nz), nz), cols]

                def emit(y, mid, total):
                    down, up = at(index + sign, y), at(index - sign, y)
                    cx = state(up, mid, down)
                    keep = pl.ds(y * nz, nz)
                    if j == 0:
                        before = state(at(index - 2 * sign, y), up, mid)
                    else:
                        before = cprev[keep]
                    if j < ppd - 1:
                        cprev[keep] = cx
                    result = mid - (total + rate_x * (cx - before))
                    sendbuf[index - 2, pl.ds(pl.multiple_of(row(y), nz), nz), cols] = result.astype(jnp.bfloat16)

                across(lambda y: at(index, y), emit)

    def own_lanes(v):
        return pl.ds(pl.multiple_of(v * width, width), width)

    def row_src(dest, h):
        return sendbuf.at[pl.ds(dest * ppd, ppd), pl.ds(pl.multiple_of(h * half, half), half)]

    def row_copy(dest, peer, r, h):
        return pltpu.make_async_remote_copy(
            src_ref=row_src(dest, h), dst_ref=recv.at[h, :, :, own_lanes(me)],
            send_sem=row_send.at[h, r], recv_sem=row_recv.at[h, r],
            device_id={"vel": peer}, device_id_type=MESH)

    def row_local(h):
        return pltpu.make_async_copy(row_src(mine, h), recv.at[h, :, :, own_lanes(me)], local_sem.at[0, h])

    def unit(dest, h):
        transport(dest, h)
        peer = vel_of(slab, dest)
        r = lax.rem(peer - me + groups, groups)

        @pl.when(r == 0)
        def _():
            row_local(h).start()

        @pl.when(r != 0)
        def _():
            row_copy(dest, peer, r, h).start()

    edge = 2 if ppd == 1 else 1
    mid_count = groups - 2 * edge
    early = mid_count // 2

    def mid_dest(k):
        return edge + lax.rem(mine + k, mid_count)

    def edge_dest(k):
        n = lax.rem(mine + k, 2 * edge)
        return n + lax.div(n, edge) * mid_count

    def row_list(h):
        out = []
        for r in range(1, groups):
            peer = lax.rem(me + r, groups)
            out.append(row_copy(chain_of(slab, peer), peer, r, h))
        return out

    def z_copies():
        return [
            pltpu.make_async_remote_copy(
                src_ref=zsend.at[pl.ds(0, 2 * plane)], dst_ref=zrecv.at[pl.ds(0, 2 * plane)],
                send_sem=z_send.at[0], recv_sem=z_recv.at[0], device_id={"space": ahead}, device_id_type=MESH),
            pltpu.make_async_remote_copy(
                src_ref=zsend.at[pl.ds(2 * plane, plane)], dst_ref=zrecv.at[pl.ds(2 * plane, plane)],
                send_sem=z_send.at[1], recv_sem=z_recv.at[1], device_id={"space": behind}, device_id_type=MESH),
        ]

    def prepare():
        own = ppd * plane
        span = 4 * LANES
        base = mine * (own // LANES)
        eye = lax.broadcasted_iota(jnp.int32, (nz, nz), 0) == lax.broadcasted_iota(jnp.int32, (nz, nz), 1)
        columns = {}
        for j in range(ppd):
            sheet = relax[mine * ppd + j]
            for h in range(HALVES):
                parts = []
                for y in range(hy):
                    line = jnp.broadcast_to(sheet[h * hy + y:h * hy + y + 1, :], (nz, nz))
                    one = jnp.sum(jnp.where(eye, line, 0.0), axis=1, keepdims=True)
                    parts.append(jnp.broadcast_to(one, (nz, LANES)))
                columns[h, j] = jnp.concatenate(parts, axis=0)
        for step in range(STEPS):
            count = counts[step, slab]
            flags = jnp.zeros((16, LANES), jnp.float32)
            for n in range(cells // span):
                which = kin_cells[step:step + 1, n * span:(n + 1) * span]
                live = n * span + lax.broadcasted_iota(jnp.int32, (1, span), 1) < count
                quotient = jnp.where(live, lax.div(which, LANES) - base, -1)
                hot_high = lax.broadcasted_iota(jnp.int32, (16, span), 0) == quotient
                hot_low = lax.broadcasted_iota(jnp.int32, (LANES, span), 0) == lax.rem(which, LANES)
                flags += lax.dot_general(
                    jnp.where(hot_high, 1.0, 0.0).astype(jnp.bfloat16), jnp.where(hot_low, 1.0, 0.0).astype(jnp.bfloat16),
                    (((1,), (1,)), ((), ())), preferred_element_type=jnp.float32)
            for j in range(ppd):
                for h in range(HALVES):
                    n = j * HALVES + h
                    kin = jnp.broadcast_to(flags[n:n + 1], (LANES, LANES)).T > 0.5
                    rate = columns[h, j]
                    here = pl.ds(j * half, half)
                    coef[step, 0, h, here] = jnp.where(kin, 1.0, 1.0 - rate)
                    coef[step, 1, h, here] = jnp.where(kin, COLLIDE, rate)
                    coef[step, 2, h, here] = jnp.where(kin, 1.0, 0.0)

    def wide(x):
        return jnp.concatenate([x] * (TILE // LANES), axis=1)

    def collide(step, h):
        rows = recv.at[h]

        def lhs():
            return rows[...].reshape(block_rows, nv)

        @pl.loop(0, rank // TILE)
        def _(n):
            cols = pl.ds(pl.multiple_of(n * TILE, TILE), TILE)
            first = jnp.dot(lhs(), map_a[:, cols], preferred_element_type=jnp.float32)
            second = jnp.dot(lhs(), map_b[:, cols], preferred_element_type=jnp.float32)
            hid[:, cols] = (first * second * wide(coef[step, 2, h])).astype(jnp.bfloat16)

        mom = jnp.dot(lhs(), basis[...], preferred_element_type=jnp.float32)
        high = mom.astype(jnp.bfloat16).astype(jnp.float32)
        is_low = (lax.broadcasted_iota(jnp.int32, mom.shape, 1) // 8) == 1
        split = jnp.where(is_low, mom - high, high)
        hid[:, rank:rank + LANES] = (split * (1.0 - coef[step, 2, h])).astype(jnp.bfloat16)

        @pl.loop(0, nv // TILE)
        def _(n):
            cols = pl.ds(pl.multiple_of(n * TILE, TILE), TILE)
            out = jnp.dot(hid[...], map_c[:, cols], preferred_element_type=jnp.float32)
            for j in range(ppd):
                part = slice(j * half, (j + 1) * half)
                here = pl.ds(h * half, half)
                if step == 0:
                    old = rows[j, :, cols].astype(jnp.float32)
                else:
                    old = mv[j, here, cols]
                new = wide(coef[step, 0, h, part]) * old + wide(coef[step, 1, h, part]) * out[part]
                if step == 0:
                    fown[j, here, cols] = new
                    fsend[h, j, :, cols] = new.astype(jnp.bfloat16)
                else:
                    outbuf[h, j, :, cols] = new.astype(jnp.bfloat16)

    low, high_part = pl.ds(0, nv // 2), pl.ds(nv // 2, nv // 2)
    whole = pl.ds(0, nv)

    def halo_copies(h):
        out = []
        for k, (j, r, lanes) in enumerate((
                (reach * ppd - 2, reach, high_part), (ppd - 1, 1, whole), (0, -1, whole), (ppd + 1 - reach * ppd, -reach, low))):
            out.append(pltpu.make_async_remote_copy(
                src_ref=fsend.at[h, j, :, lanes], dst_ref=halo.at[h, k, :, lanes],
                send_sem=halo_send.at[h, k], recv_sem=halo_recv.at[h, k],
                device_id=along(r), device_id_type=MESH))
        return out

    def sideways(h):
        @pl.loop(0, nv // LANES)
        def _(t):
            cols = pl.ds(pl.multiple_of(t * LANES, LANES), LANES)
            for j in range(ppd):
                def emit(y, mid, total):
                    mv[j, pl.ds((h * hy + y) * nz, nz), cols] = mid - total

                across(lambda y: fown[j, pl.ds(((h * hy + y) % ny) * nz, nz), cols], emit)

    def forward(h):
        half_tiles = nv // LANES // 2
        for up in (-1, 1):
            @pl.loop(0, half_tiles)
            def _(n):
                t = n + (half_tiles if up > 0 else 0)
                cols = pl.ds(pl.multiple_of(t * LANES, LANES), LANES)
                rate_x = speed(t)

                def value(k, y):
                    here = pl.ds(y * nz, nz)
                    if 0 <= k < ppd:
                        return fown[k, pl.ds((h * hy + y) * nz, nz), cols]
                    slot = k + 2 if k < 0 else k - ppd + 2
                    return halo[h, slot, here, cols].astype(jnp.float32)

                order = list(range(ppd)) if up > 0 else list(range(ppd - 1, -1, -1))
                for y in range(hy):
                    line = [order[0] - 2 * up, order[0] - up] + order + [order[-1] + up]
                    f = [value(k, y) for k in line]
                    c = [state(f[n], f[n + 1], f[n + 2]) for n in range(ppd + 1)]
                    here = pl.ds((h * hy + y) * nz, nz)
                    for n, j in enumerate(order):
                        result = mv[j, here, cols] - rate_x * (c[n + 1] - c[n])
                        mv[j, here, cols] = result
                        recv[h, j, pl.ds(y * nz, nz), cols] = result.astype(jnp.bfloat16)

    def res_copies(h):
        out = []
        for r in range(1, groups):
            peer = lax.rem(me + r, groups)
            out.append(pltpu.make_async_remote_copy(
                src_ref=outbuf.at[h, :, :, own_lanes(peer)],
                dst_ref=ret_out.at[pl.ds(mine * ppd, ppd), pl.ds(h * half, half)],
                send_sem=res_send.at[h, r], recv_sem=res_recv.at[h, r],
                device_id={"vel": peer}, device_id_type=MESH))
        return out

    def res_local(h):
        return pltpu.make_async_copy(
            outbuf.at[h, :, :, own_lanes(me)],
            ret_out.at[pl.ds(mine * ppd, ppd), pl.ds(h * half, half)], local_sem.at[1, h])

    for copy in loads:
        copy.wait()
    two, one = 2 * plane, plane
    zsend[pl.ds(0, two)] = cur[pl.ds(pl.multiple_of(pick(nx * plane, two), plane), two)].astype(jnp.bfloat16)
    zsend[pl.ds(two, one)] = cur[pl.ds(pl.multiple_of(pick(two, (nx + 1) * plane), plane), one)].astype(jnp.bfloat16)
    z_list = z_copies()
    for copy in z_list:
        copy.start()

    @pl.loop(0, mid_count + early)
    def _(k):
        h = lax.div(k, mid_count)
        unit(mid_dest(k - h * mid_count), h)

    prepare()
    for copy in z_list:
        copy.wait_recv()
    cur[pl.ds(pl.multiple_of(pick(0, (nx + 2) * plane), plane), two)] = zrecv[pl.ds(0, two)].astype(jnp.float32)
    cur[pl.ds(pl.multiple_of(pick((nx + 2) * plane, plane), plane), one)] = zrecv[pl.ds(two, one)].astype(jnp.float32)

    @pl.loop(0, 4 * edge + mid_count - early)
    def _(k):
        h = jnp.where(k < 2 * edge, 0, 1)
        n = k - h * 2 * edge
        rest = mid_count - early
        at_mid = h * jnp.where(n < rest, 1, 0)
        e = n - h * rest
        dest = at_mid * mid_dest(early + n) + (1 - at_mid) * edge_dest(e + 2 * edge * at_mid + rest * at_mid)
        unit(dest, h)

    for copy in consts:
        copy.wait()
    rows_in = [row_list(h) for h in range(HALVES)]
    halos = [halo_copies(h) for h in range(HALVES)]
    results = [res_copies(h) for h in range(HALVES)]
    for h in range(HALVES):
        for copy in rows_in[h]:
            copy.wait_recv()
        row_local(h).wait()
        collide(0, h)
        for copy in halos[h]:
            copy.start()
    for h in range(HALVES):
        sideways(h)
        for copy in halos[h]:
            copy.wait_recv()
        forward(h)
        collide(1, h)
        for copy in results[h]:
            copy.start()
        res_local(h).start()
    for copy in z_list:
        copy.wait_send()
    for h in range(HALVES):
        for copy in rows_in[h] + halos[h]:
            copy.wait_send()
        for copy in results[h]:
            copy.wait()
        res_local(h).wait()


def body(dist, relax_rate, kinetic_cells, kinetic_count, map_a, map_b, map_c):
    nx, ny, nz, width = dist.shape
    groups = lax.axis_size("vel")
    slabs = lax.axis_size("space")
    cells = nx * ny * nz
    plane = ny * nz
    nv = groups * width
    rank = map_a.shape[1]
    ppd = nx // groups
    half = plane // HALVES
    basis, back = tables()

    any_space = pl.BlockSpec(memory_space=pl.ANY)
    f32, bf16 = jnp.float32, jnp.bfloat16
    dims = (nx, ny, nz, width, groups, slabs)
    vmem = pl.BlockSpec(memory_space=pltpu.VMEM)
    dma = pltpu.SemaphoreType.DMA
    ret = pl.pallas_call(
        functools.partial(kernel, dims),
        out_shape=jax.ShapeDtypeStruct((nx, plane, width), bf16),
        in_specs=[pl.BlockSpec(memory_space=pltpu.SMEM)] + [vmem] * 2 + [any_space] * 6,
        out_specs=any_space,
        scratch_shapes=[
            pltpu.VMEM(((nx + 4) * plane, width), f32),
            pltpu.VMEM((half, LANES), f32),
            pltpu.VMEM((nx, plane, width), bf16),
            pltpu.VMEM((3 * plane, width), bf16),
            pltpu.VMEM((3 * plane, width), bf16),
            pltpu.VMEM((HALVES, ppd, half, nv), bf16),
            pltpu.VMEM((ppd, plane, nv), f32),
            pltpu.VMEM((HALVES, ppd, half, nv), bf16),
            pltpu.VMEM((HALVES, 4, half, nv), bf16),
            pltpu.VMEM((ppd, plane, nv), f32),
            pltpu.VMEM((HALVES, ppd, half, nv), bf16),
            pltpu.VMEM(map_a.shape, bf16),
            pltpu.VMEM(map_b.shape, bf16),
            pltpu.VMEM((rank + LANES, nv), bf16),
            pltpu.VMEM((nv, LANES), bf16),
            pltpu.VMEM((ppd * half, rank + LANES), bf16),
            pltpu.VMEM((STEPS, 3, HALVES, ppd * half, LANES), f32),
            dma((4,)),
            dma((5,)),
            dma((2, HALVES)),
            dma((2,)),
            dma((2,)),
            dma((HALVES, groups)),
            dma((HALVES, groups)),
            dma((HALVES, 4)),
            dma((HALVES, 4)),
            dma((HALVES, groups)),
            dma((HALVES, groups)),
        ],
        compiler_params=pltpu.CompilerParams(
            collective_id=0, has_side_effects=True, vmem_limit_bytes=67043328),
    )(kinetic_count, kinetic_cells, relax_rate, dist.reshape(cells, width), map_a, map_b, map_c,
      jnp.asarray(basis), jnp.asarray(back))
    return ret.reshape(dist.shape).astype(f32)


def solution(mesh):
    return jax.shard_map(
        body,
        mesh=mesh,
        in_specs=(
            P("space", None, None, "vel"),
            P("space", None, None),
            P(None, "space"),
            P(),
            P(),
            P(),
            P(),
        ),
        out_specs=P("space", None, None, "vel"),
        check_vma=False,
    )
```

```python
import functools

import jax
import jax.numpy as jnp
import numpy as np
from jax import lax
from jax.experimental import pallas as pl
from jax.experimental.pallas import tpu as pltpu
from jax.sharding import PartitionSpec as P

GX = 16
GY = 16
GZ = 8
STEPS = 2
COURANT = 0.1
SPACING = 0.5
COLLIDE = 0.5
LANES = 128
TILE = 256
HALVES = 2
MESH = pl.DeviceIdType.MESH


def tables():
    k = np.arange(GX * GY * GZ)
    vx = ((k // (GY * GZ)) - 0.5 * (GX - 1)) * SPACING
    vy = (((k // GZ) % GY) - 0.5 * (GY - 1)) * SPACING
    vz = ((k % GZ) - 0.5 * (GZ - 1)) * SPACING
    s = vx * vx + vy * vy + vz * vz
    w = np.exp(-0.5 * s)
    w = w / w.sum()
    m2, m4 = (w * s).sum(), (w * s * s).sum()
    kappa = m4 - m2 * m2
    per_e = w * (s - m2) / kappa
    rows = np.stack([
        w - m2 * per_e,
        w * vx / (w * vx * vx).sum(),
        w * vy / (w * vy * vy).sum(),
        w * vz / (w * vz * vz).sum(),
        per_e,
        per_e,
    ])
    s_hi = np.asarray(np.asarray(s, np.float32).astype(jnp.bfloat16), np.float64)
    cols = np.stack([np.ones_like(vx), vx, vy, vz, s_hi, s - s_hi], axis=1)
    g_hi = np.asarray(np.asarray(rows, np.float32).astype(jnp.bfloat16), np.float64)
    g_lo = rows - g_hi
    basis = np.zeros((k.size, LANES))
    back = np.zeros((LANES, k.size))
    for at, part in ((0, g_hi), (8, g_hi), (16, g_lo)):
        basis[:, at:at + 6] = cols
        back[at:at + 6] = part
    return basis.astype(np.float32).astype(jnp.bfloat16), back.astype(np.float32).astype(jnp.bfloat16)


def limited(a, b):
    return jnp.minimum(jnp.maximum(a, jnp.minimum(b, 0.0)), jnp.maximum(b, 0.0))


def state(up, mid, down):
    return mid + 0.5 * limited(mid - up, down - mid)


def kernel(dims, counts, kin_cells, relax, dist, a_hbm, b_hbm, c_hbm, basis_hbm, back_hbm,
           ret_out,
           cur, cprev, sendbuf, zsend, zrecv, recv, fown, fsend, halo, mv, outbuf,
           map_a, map_b, map_c, basis, hid, coef,
           load_sem, const_sem, local_sem, z_send, z_recv, row_send, row_recv, halo_send, halo_recv, res_send, res_recv):
    nx, ny, nz, width, groups, slabs = dims
    plane = ny * nz
    cells = nx * plane
    nv = groups * width
    rank = map_a.shape[1]
    ppd = nx // groups
    hy = ny // HALVES
    half = hy * nz
    block_rows = ppd * half
    tiles = width // LANES
    nchips = groups // 2
    ncol = groups // 4
    me = lax.axis_index("vel")
    slab = lax.axis_index("space")
    first_x = lax.div(me * width, GY * GZ)
    bit = lax.div(first_x, GX // 2)
    sign = 2 * bit - 1
    ahead = lax.rem(slab + sign + slabs, slabs)
    behind = lax.rem(slab - sign + slabs, slabs)

    def vel_of(s, p):
        q = lax.rem(lax.div(p, 2) + nchips * slabs - s, nchips)
        y = lax.div(q, ncol)
        x = lax.rem(q, ncol)
        return (y * ncol + x + y * (ncol - 1 - 2 * x)) * 2 + lax.rem(p, 2)

    def chain_of(s, v):
        chip = lax.div(v, 2)
        y = lax.div(chip, ncol)
        x = lax.rem(chip, ncol)
        q = y * ncol + x + y * (ncol - 1 - 2 * x)
        return 2 * lax.rem(q + s, nchips) + lax.rem(v, 2)

    mine = chain_of(slab, me)

    def along(r):
        at = mine + r + groups
        s = lax.rem(slab + lax.div(at, groups) - 1 + slabs, slabs)
        return {"space": s, "vel": vel_of(s, lax.rem(at, groups))}

    pieces = 4
    loads = []
    for n, c in enumerate((0, pieces - 1) + tuple(range(1, pieces - 1))):
        size = cells // pieces
        loads.append(pltpu.make_async_copy(
            dist.at[pl.ds(c * size, size)], cur.at[pl.ds(2 * plane + c * size, size)], load_sem.at[n]))
        loads[-1].start()
    consts = []
    for n, (src, dst) in enumerate(((a_hbm, map_a), (b_hbm, map_b), (c_hbm, map_c.at[pl.ds(0, rank)]),
                                    (back_hbm, map_c.at[pl.ds(rank, LANES)]), (basis_hbm, basis))):
        consts.append(pltpu.make_async_copy(src, dst, const_sem.at[n]))

    reach = 1 if ppd > 1 else 2
    barrier = pltpu.get_barrier_semaphore()
    for p in range(1, groups):
        pl.semaphore_signal(barrier, inc=1, device_id={"vel": lax.rem(me + p, groups)}, device_id_type=MESH)
    pl.semaphore_signal(barrier, inc=1, device_id={"space": ahead}, device_id_type=MESH)
    pl.semaphore_signal(barrier, inc=1, device_id={"space": behind}, device_id_type=MESH)
    for r in range(1, reach + 1):
        pl.semaphore_signal(barrier, inc=1, device_id=along(r), device_id_type=MESH)
        pl.semaphore_signal(barrier, inc=1, device_id=along(-r), device_id_type=MESH)

    lane = lax.broadcasted_iota(jnp.int32, (1, LANES), 1)
    vy = (((lane // GZ) % GY).astype(jnp.float32) - 0.5 * (GY - 1)) * SPACING
    vz = ((lane % GZ).astype(jnp.float32) - 0.5 * (GZ - 1)) * SPACING
    block = (nz, LANES)
    pos_y = jnp.broadcast_to(vy > 0.0, block)
    pos_z = jnp.broadcast_to(vz > 0.0, block)
    half_y = jnp.broadcast_to(jnp.where(vy > 0.0, 0.5, -0.5), block)
    half_z = jnp.broadcast_to(jnp.where(vz > 0.0, 0.5, -0.5), block)
    rate_y = jnp.broadcast_to(COURANT * jnp.abs(vy), block)
    rate_z = jnp.broadcast_to(COURANT * jnp.abs(vz), block)

    def pick(positive, negative):
        return bit * positive + (1 - bit) * negative

    def across(value, emit):
        def y_state(mid, before, after):
            return mid + half_y * limited(before, after)

        f = {y: value(y) for y in range(-2, 2)}
        d = {y: f[y + 1] - f[y] for y in (-2, -1, 0)}
        cy = {y: y_state(f[y], d[y - 1], d[y]) for y in (-1, 0)}
        for y in range(hy):
            f[y + 2] = value(y + 2)
            d[y + 1] = f[y + 2] - f[y + 1]
            cy[y + 1] = y_state(f[y + 1], d[y], d[y + 1])
            mid = f[y]
            total = rate_y * (cy[y] - jnp.where(pos_y, cy[y - 1], cy[y + 1]))
            dz = pltpu.roll(mid, nz - 1, 0) - mid
            cz = mid + half_z * limited(pltpu.roll(dz, 1, 0), dz)
            total += rate_z * (cz - jnp.where(pos_z, pltpu.roll(cz, 1, 0), pltpu.roll(cz, nz - 1, 0)))
            emit(y, mid, total)

    def speed(tile):
        return COURANT * jnp.abs((tile.astype(jnp.float32) - 0.5 * (GX - 1)) * SPACING)

    def transport(dest, h):
        def row(y):
            return lax.rem(h * hy + y + ny, ny) * nz

        @pl.loop(0, tiles)
        def _(t):
            cols = pl.ds(pl.multiple_of(t * LANES, LANES), LANES)
            rate_x = speed(lax.div(me * width + t * LANES, GY * GZ))
            for j in range(ppd):
                index = 2 + dest * ppd + pick(j, ppd - 1 - j)

                def at(k, y):
                    return cur[pl.ds(pl.multiple_of(k * plane + row(y), nz), nz), cols]

                def emit(y, mid, total):
                    down, up = at(index + sign, y), at(index - sign, y)
                    cx = state(up, mid, down)
                    keep = pl.ds(y * nz, nz)
                    if j == 0:
                        before = state(at(index - 2 * sign, y), up, mid)
                    else:
                        before = cprev[keep]
                    if j < ppd - 1:
                        cprev[keep] = cx
                    result = mid - (total + rate_x * (cx - before))
                    sendbuf[index - 2, pl.ds(pl.multiple_of(row(y), nz), nz), cols] = result.astype(jnp.bfloat16)

                across(lambda y: at(index, y), emit)

    def own_lanes(v):
        return pl.ds(pl.multiple_of(v * width, width), width)

    def row_src(dest, h):
        return sendbuf.at[pl.ds(dest * ppd, ppd), pl.ds(pl.multiple_of(h * half, half), half)]

    def row_copy(dest, peer, r, h):
        return pltpu.make_async_remote_copy(
            src_ref=row_src(dest, h), dst_ref=recv.at[h, :, :, own_lanes(me)],
            send_sem=row_send.at[h, r], recv_sem=row_recv.at[h, r],
            device_id={"vel": peer}, device_id_type=MESH)

    def row_local(h):
        return pltpu.make_async_copy(row_src(mine, h), recv.at[h, :, :, own_lanes(me)], local_sem.at[0, h])

    def unit(dest, h):
        transport(dest, h)
        peer = vel_of(slab, dest)
        r = lax.rem(peer - me + groups, groups)

        @pl.when(r == 0)
        def _():
            row_local(h).start()

        @pl.when(r != 0)
        def _():
            row_copy(dest, peer, r, h).start()

    edge = 2 if ppd == 1 else 1
    mid_count = groups - 2 * edge
    far_count = groups - 4 * edge

    def mid_dest(k):
        return edge + lax.rem(mine + k, mid_count)

    def edge_dest(k):
        n = lax.rem(mine + k, 2 * edge)
        return n + lax.div(n, edge) * mid_count

    def near_dest(k):
        n = lax.rem(mine + k, 2 * edge)
        return edge + n + lax.div(n, edge) * far_count

    def late_dest(k):
        n = lax.rem(mine + k, mid_count)
        first = jnp.where(n < edge, 1, 0)
        last = jnp.where(n >= mid_count - edge, 1, 0)
        return first * n + last * (n + 2 * edge) + (1 - first - last) * (n + edge)

    def row_list(h):
        out = []
        for r in range(1, groups):
            peer = lax.rem(me + r, groups)
            out.append(row_copy(chain_of(slab, peer), peer, r, h))
        return out

    def z_copies():
        return [
            pltpu.make_async_remote_copy(
                src_ref=zsend.at[pl.ds(0, 2 * plane)], dst_ref=zrecv.at[pl.ds(0, 2 * plane)],
                send_sem=z_send.at[0], recv_sem=z_recv.at[0], device_id={"space": ahead}, device_id_type=MESH),
            pltpu.make_async_remote_copy(
                src_ref=zsend.at[pl.ds(2 * plane, plane)], dst_ref=zrecv.at[pl.ds(2 * plane, plane)],
                send_sem=z_send.at[1], recv_sem=z_recv.at[1], device_id={"space": behind}, device_id_type=MESH),
        ]

    def prepare():
        own = ppd * plane
        span = 4 * LANES
        base = mine * (own // LANES)
        eye = lax.broadcasted_iota(jnp.int32, (nz, nz), 0) == lax.broadcasted_iota(jnp.int32, (nz, nz), 1)
        columns = {}
        for j in range(ppd):
            sheet = relax[mine * ppd + j]
            for h in range(HALVES):
                parts = []
                for y in range(hy):
                    line = jnp.broadcast_to(sheet[h * hy + y:h * hy + y + 1, :], (nz, nz))
                    one = jnp.sum(jnp.where(eye, line, 0.0), axis=1, keepdims=True)
                    parts.append(jnp.broadcast_to(one, (nz, LANES)))
                columns[h, j] = jnp.concatenate(parts, axis=0)
        for step in range(STEPS):
            count = counts[step, slab]
            flags = jnp.zeros((16, LANES), jnp.float32)
            for n in range(cells // span):
                which = kin_cells[step:step + 1, n * span:(n + 1) * span]
                live = n * span + lax.broadcasted_iota(jnp.int32, (1, span), 1) < count
                quotient = jnp.where(live, lax.div(which, LANES) - base, -1)
                hot_high = lax.broadcasted_iota(jnp.int32, (16, span), 0) == quotient
                hot_low = lax.broadcasted_iota(jnp.int32, (LANES, span), 0) == lax.rem(which, LANES)
                flags += lax.dot_general(
                    jnp.where(hot_high, 1.0, 0.0).astype(jnp.bfloat16), jnp.where(hot_low, 1.0, 0.0).astype(jnp.bfloat16),
                    (((1,), (1,)), ((), ())), preferred_element_type=jnp.float32)
            for j in range(ppd):
                for h in range(HALVES):
                    n = j * HALVES + h
                    kin = jnp.broadcast_to(flags[n:n + 1], (LANES, LANES)).T > 0.5
                    rate = columns[h, j]
                    here = pl.ds(j * half, half)
                    coef[step, 0, h, here] = jnp.where(kin, 1.0, 1.0 - rate)
                    coef[step, 1, h, here] = jnp.where(kin, COLLIDE, rate)
                    coef[step, 2, h, here] = jnp.where(kin, 1.0, 0.0)

    def wide(x):
        return jnp.concatenate([x] * (TILE // LANES), axis=1)

    def collide(step, h):
        rows = recv.at[h]

        def lhs():
            return rows[...].reshape(block_rows, nv)

        @pl.loop(0, rank // TILE)
        def _(n):
            cols = pl.ds(pl.multiple_of(n * TILE, TILE), TILE)
            first = jnp.dot(lhs(), map_a[:, cols], preferred_element_type=jnp.float32)
            second = jnp.dot(lhs(), map_b[:, cols], preferred_element_type=jnp.float32)
            hid[:, cols] = (first * second * wide(coef[step, 2, h])).astype(jnp.bfloat16)

        mom = jnp.dot(lhs(), basis[...], preferred_element_type=jnp.float32)
        high = mom.astype(jnp.bfloat16).astype(jnp.float32)
        is_low = (lax.broadcasted_iota(jnp.int32, mom.shape, 1) // 8) == 1
        split = jnp.where(is_low, mom - high, high)
        hid[:, rank:rank + LANES] = (split * (1.0 - coef[step, 2, h])).astype(jnp.bfloat16)

        @pl.loop(0, nv // TILE)
        def _(n):
            cols = pl.ds(pl.multiple_of(n * TILE, TILE), TILE)
            out = jnp.dot(hid[...], map_c[:, cols], preferred_element_type=jnp.float32)
            for j in range(ppd):
                part = slice(j * half, (j + 1) * half)
                here = pl.ds(h * half, half)
                if step == 0:
                    old = rows[j, :, cols].astype(jnp.float32)
                else:
                    old = mv[j, here, cols]
                new = wide(coef[step, 0, h, part]) * old + wide(coef[step, 1, h, part]) * out[part]
                if step == 0:
                    fown[j, here, cols] = new
                    fsend[h, j, :, cols] = new.astype(jnp.bfloat16)
                else:
                    outbuf[h, j, :, cols] = new.astype(jnp.bfloat16)

    low, high_part = pl.ds(0, nv // 2), pl.ds(nv // 2, nv // 2)
    whole = pl.ds(0, nv)

    def halo_copies(h):
        out = []
        for k, (j, r, lanes) in enumerate((
                (reach * ppd - 2, reach, high_part), (ppd - 1, 1, whole), (0, -1, whole), (ppd + 1 - reach * ppd, -reach, low))):
            out.append(pltpu.make_async_remote_copy(
                src_ref=fsend.at[h, j, :, lanes], dst_ref=halo.at[h, k, :, lanes],
                send_sem=halo_send.at[h, k], recv_sem=halo_recv.at[h, k],
                device_id=along(r), device_id_type=MESH))
        return out

    def sideways(h):
        @pl.loop(0, nv // LANES)
        def _(t):
            cols = pl.ds(pl.multiple_of(t * LANES, LANES), LANES)
            for j in range(ppd):
                def emit(y, mid, total):
                    mv[j, pl.ds((h * hy + y) * nz, nz), cols] = mid - total

                across(lambda y: fown[j, pl.ds(((h * hy + y) % ny) * nz, nz), cols], emit)

    def forward(h):
        half_tiles = nv // LANES // 2
        for up in (-1, 1):
            @pl.loop(0, half_tiles)
            def _(n):
                t = n + (half_tiles if up > 0 else 0)
                cols = pl.ds(pl.multiple_of(t * LANES, LANES), LANES)
                rate_x = speed(t)

                def value(k, y):
                    here = pl.ds(y * nz, nz)
                    if 0 <= k < ppd:
                        return fown[k, pl.ds((h * hy + y) * nz, nz), cols]
                    slot = k + 2 if k < 0 else k - ppd + 2
                    return halo[h, slot, here, cols].astype(jnp.float32)

                order = list(range(ppd)) if up > 0 else list(range(ppd - 1, -1, -1))
                for y in range(hy):
                    line = [order[0] - 2 * up, order[0] - up] + order + [order[-1] + up]
                    f = [value(k, y) for k in line]
                    c = [state(f[n], f[n + 1], f[n + 2]) for n in range(ppd + 1)]
                    here = pl.ds((h * hy + y) * nz, nz)
                    for n, j in enumerate(order):
                        result = mv[j, here, cols] - rate_x * (c[n + 1] - c[n])
                        mv[j, here, cols] = result
                        recv[h, j, pl.ds(y * nz, nz), cols] = result.astype(jnp.bfloat16)

    def res_copies(h):
        out = []
        for r in range(1, groups):
            peer = lax.rem(me + r, groups)
            out.append(pltpu.make_async_remote_copy(
                src_ref=outbuf.at[h, :, :, own_lanes(peer)],
                dst_ref=ret_out.at[pl.ds(mine * ppd, ppd), pl.ds(h * half, half)],
                send_sem=res_send.at[h, r], recv_sem=res_recv.at[h, r],
                device_id={"vel": peer}, device_id_type=MESH))
        return out

    def res_local(h):
        return pltpu.make_async_copy(
            outbuf.at[h, :, :, own_lanes(me)],
            ret_out.at[pl.ds(mine * ppd, ppd), pl.ds(h * half, half)], local_sem.at[1, h])

    for copy in loads[:2]:
        copy.wait()
    two, one = 2 * plane, plane
    zsend[pl.ds(0, two)] = cur[pl.ds(pl.multiple_of(pick(nx * plane, two), plane), two)].astype(jnp.bfloat16)
    zsend[pl.ds(two, one)] = cur[pl.ds(pl.multiple_of(pick(two, (nx + 1) * plane), plane), one)].astype(jnp.bfloat16)
    z_list = z_copies()
    pl.semaphore_wait(barrier, groups + 1 + 2 * reach)
    for copy in z_list:
        copy.start()
    for copy in loads[2:]:
        copy.wait()
    for copy in consts:
        copy.start()

    @pl.loop(0, mid_count + 2 * edge)
    def _(k):
        h = lax.div(k, mid_count)
        unit((1 - h) * mid_dest(k) + h * near_dest(k), h)

    prepare()
    for copy in z_list:
        copy.wait_recv()
    cur[pl.ds(pl.multiple_of(pick(0, (nx + 2) * plane), plane), two)] = zrecv[pl.ds(0, two)].astype(jnp.float32)
    cur[pl.ds(pl.multiple_of(pick((nx + 2) * plane, plane), plane), one)] = zrecv[pl.ds(two, one)].astype(jnp.float32)

    @pl.loop(0, mid_count + 2 * edge)
    def _(k):
        h = jnp.where(k < 2 * edge, 0, 1)
        unit((1 - h) * edge_dest(k) + h * late_dest(k), h)

    for copy in consts:
        copy.wait()
    rows_in = [row_list(h) for h in range(HALVES)]
    halos = [halo_copies(h) for h in range(HALVES)]
    results = [res_copies(h) for h in range(HALVES)]
    for h in range(HALVES):
        for copy in rows_in[h]:
            copy.wait_recv()
        row_local(h).wait()
        collide(0, h)
        for copy in halos[h]:
            copy.start()
    for h in range(HALVES):
        sideways(h)
        for copy in halos[h]:
            copy.wait_recv()
        forward(h)
        collide(1, h)
        for copy in results[h]:
            copy.start()
        res_local(h).start()
    for copy in z_list:
        copy.wait_send()
    for h in range(HALVES):
        for copy in rows_in[h] + halos[h]:
            copy.wait_send()
        for copy in results[h]:
            copy.wait()
        res_local(h).wait()


def body(dist, relax_rate, kinetic_cells, kinetic_count, map_a, map_b, map_c):
    nx, ny, nz, width = dist.shape
    groups = lax.axis_size("vel")
    slabs = lax.axis_size("space")
    cells = nx * ny * nz
    plane = ny * nz
    nv = groups * width
    rank = map_a.shape[1]
    ppd = nx // groups
    half = plane // HALVES
    basis, back = tables()

    any_space = pl.BlockSpec(memory_space=pl.ANY)
    f32, bf16 = jnp.float32, jnp.bfloat16
    dims = (nx, ny, nz, width, groups, slabs)
    vmem = pl.BlockSpec(memory_space=pltpu.VMEM)
    dma = pltpu.SemaphoreType.DMA
    ret = pl.pallas_call(
        functools.partial(kernel, dims),
        out_shape=jax.ShapeDtypeStruct((nx, plane, width), bf16),
        in_specs=[pl.BlockSpec(memory_space=pltpu.SMEM)] + [vmem] * 2 + [any_space] * 6,
        out_specs=any_space,
        scratch_shapes=[
            pltpu.VMEM(((nx + 4) * plane, width), f32),
            pltpu.VMEM((half, LANES), f32),
            pltpu.VMEM((nx, plane, width), bf16),
            pltpu.VMEM((3 * plane, width), bf16),
            pltpu.VMEM((3 * plane, width), bf16),
            pltpu.VMEM((HALVES, ppd, half, nv), bf16),
            pltpu.VMEM((ppd, plane, nv), f32),
            pltpu.VMEM((HALVES, ppd, half, nv), bf16),
            pltpu.VMEM((HALVES, 4, half, nv), bf16),
            pltpu.VMEM((ppd, plane, nv), f32),
            pltpu.VMEM((HALVES, ppd, half, nv), bf16),
            pltpu.VMEM(map_a.shape, bf16),
            pltpu.VMEM(map_b.shape, bf16),
            pltpu.VMEM((rank + LANES, nv), bf16),
            pltpu.VMEM((nv, LANES), bf16),
            pltpu.VMEM((ppd * half, rank + LANES), bf16),
            pltpu.VMEM((STEPS, 3, HALVES, ppd * half, LANES), f32),
            dma((4,)),
            dma((5,)),
            dma((2, HALVES)),
            dma((2,)),
            dma((2,)),
            dma((HALVES, groups)),
            dma((HALVES, groups)),
            dma((HALVES, 4)),
            dma((HALVES, 4)),
            dma((HALVES, groups)),
            dma((HALVES, groups)),
        ],
        compiler_params=pltpu.CompilerParams(
            collective_id=0, has_side_effects=True, vmem_limit_bytes=67043328),
    )(kinetic_count, kinetic_cells, relax_rate, dist.reshape(cells, width), map_a, map_b, map_c,
      jnp.asarray(basis), jnp.asarray(back))
    parts = 16
    out = pl.pallas_call(
        widen,
        out_shape=jax.ShapeDtypeStruct((cells, width), f32),
        in_specs=[any_space],
        out_specs=any_space,
        scratch_shapes=[
            pltpu.VMEM((parts, cells // parts, width), bf16),
            pltpu.VMEM((parts, cells // parts, width), f32),
            dma((parts,)),
            dma((parts,)),
        ],
    )(ret.reshape(cells, width))
    return out.reshape(dist.shape)


def widen(src, out, buf, wide_buf, in_sem, out_sem):
    parts = in_sem.shape[0]
    size = src.shape[0] // parts
    ins = [pltpu.make_async_copy(src.at[pl.ds(n * size, size)], buf.at[n], in_sem.at[n]) for n in range(parts)]
    outs = [pltpu.make_async_copy(wide_buf.at[n], out.at[pl.ds(n * size, size)], out_sem.at[n]) for n in range(parts)]
    for copy in ins:
        copy.start()
    for n in range(parts):
        ins[n].wait()
        wide_buf[n] = buf[n].astype(jnp.float32)
        outs[n].start()
    for copy in outs:
        copy.wait()


def solution(mesh):
    return jax.shard_map(
        body,
        mesh=mesh,
        in_specs=(
            P("space", None, None, "vel"),
            P("space", None, None),
            P(None, "space"),
            P(),
            P(),
            P(),
            P(),
        ),
        out_specs=P("space", None, None, "vel"),
        check_vma=False,
    )
```

```python
import functools

import jax
import jax.numpy as jnp
import numpy as np
from jax import lax
from jax.experimental import pallas as pl
from jax.experimental.pallas import tpu as pltpu
from jax.sharding import PartitionSpec as P

GX = 16
GY = 16
GZ = 8
STEPS = 2
COURANT = 0.1
SPACING = 0.5
COLLIDE = 0.5
LANES = 128
TILE = 256
HALVES = 2
MESH = pl.DeviceIdType.MESH


def tables():
    k = np.arange(GX * GY * GZ)
    vx = ((k // (GY * GZ)) - 0.5 * (GX - 1)) * SPACING
    vy = (((k // GZ) % GY) - 0.5 * (GY - 1)) * SPACING
    vz = ((k % GZ) - 0.5 * (GZ - 1)) * SPACING
    s = vx * vx + vy * vy + vz * vz
    w = np.exp(-0.5 * s)
    w = w / w.sum()
    m2, m4 = (w * s).sum(), (w * s * s).sum()
    kappa = m4 - m2 * m2
    per_e = w * (s - m2) / kappa
    rows = np.stack([
        w - m2 * per_e,
        w * vx / (w * vx * vx).sum(),
        w * vy / (w * vy * vy).sum(),
        w * vz / (w * vz * vz).sum(),
        per_e,
        per_e,
    ])
    s_hi = np.asarray(np.asarray(s, np.float32).astype(jnp.bfloat16), np.float64)
    cols = np.stack([np.ones_like(vx), vx, vy, vz, s_hi, s - s_hi], axis=1)
    g_hi = np.asarray(np.asarray(rows, np.float32).astype(jnp.bfloat16), np.float64)
    g_lo = rows - g_hi
    basis = np.zeros((k.size, LANES))
    back = np.zeros((LANES, k.size))
    for at, part in ((0, g_hi), (8, g_hi), (16, g_lo)):
        basis[:, at:at + 6] = cols
        back[at:at + 6] = part
    return basis.astype(np.float32).astype(jnp.bfloat16), back.astype(np.float32).astype(jnp.bfloat16)


def limited(a, b):
    return jnp.minimum(jnp.maximum(a, jnp.minimum(b, 0.0)), jnp.maximum(b, 0.0))


def state(up, mid, down):
    return mid + 0.5 * limited(mid - up, down - mid)


def kernel(dims, counts_hbm, kin_hbm, relax_hbm, dist, a_hbm, b_hbm, c_hbm, basis_hbm, back_hbm,
           ret_out,
           cur, cprev, sendbuf, zsend, zrecv, recv, fown, fsend, halo, mv, outbuf,
           map_a, map_b, map_c, basis, hid, coef, counts, kin_cells, relax,
           load_sem, const_sem, local_sem, z_send, z_recv, row_send, row_recv, halo_send, halo_recv, res_send, res_recv):
    nx, ny, nz, width, groups, slabs = dims
    plane = ny * nz
    cells = nx * plane
    nv = groups * width
    rank = map_a.shape[1]
    ppd = nx // groups
    hy = ny // HALVES
    half = hy * nz
    block_rows = ppd * half
    tiles = width // LANES
    nchips = groups // 2
    ncol = groups // 4
    me = lax.axis_index("vel")
    slab = lax.axis_index("space")
    first_x = lax.div(me * width, GY * GZ)
    bit = lax.div(first_x, GX // 2)
    sign = 2 * bit - 1
    ahead = lax.rem(slab + sign + slabs, slabs)
    behind = lax.rem(slab - sign + slabs, slabs)

    def vel_of(s, p):
        q = lax.rem(lax.div(p, 2) + nchips * slabs - s, nchips)
        y = lax.div(q, ncol)
        x = lax.rem(q, ncol)
        return (y * ncol + x + y * (ncol - 1 - 2 * x)) * 2 + lax.rem(p, 2)

    def chain_of(s, v):
        chip = lax.div(v, 2)
        y = lax.div(chip, ncol)
        x = lax.rem(chip, ncol)
        q = y * ncol + x + y * (ncol - 1 - 2 * x)
        return 2 * lax.rem(q + s, nchips) + lax.rem(v, 2)

    mine = chain_of(slab, me)

    def along(r):
        at = mine + r + groups
        s = lax.rem(slab + lax.div(at, groups) - 1 + slabs, slabs)
        return {"space": s, "vel": vel_of(s, lax.rem(at, groups))}

    reach = 1 if ppd > 1 else 2
    barrier = pltpu.get_barrier_semaphore()
    for p in range(1, groups):
        pl.semaphore_signal(barrier, inc=1, device_id={"vel": lax.rem(me + p, groups)}, device_id_type=MESH)
    pl.semaphore_signal(barrier, inc=1, device_id={"space": ahead}, device_id_type=MESH)
    pl.semaphore_signal(barrier, inc=1, device_id={"space": behind}, device_id_type=MESH)
    for r in range(1, reach + 1):
        pl.semaphore_signal(barrier, inc=1, device_id=along(r), device_id_type=MESH)
        pl.semaphore_signal(barrier, inc=1, device_id=along(-r), device_id_type=MESH)

    pieces = 4
    loads = []
    for n, c in enumerate((0, pieces - 1) + tuple(range(1, pieces - 1))):
        size = cells // pieces
        loads.append(pltpu.make_async_copy(
            dist.at[pl.ds(c * size, size)], cur.at[pl.ds(2 * plane + c * size, size)], load_sem.at[n]))
        loads[-1].start()
    consts = []
    for n, (src, dst) in enumerate(((a_hbm, map_a), (b_hbm, map_b), (c_hbm, map_c.at[pl.ds(0, rank)]),
                                    (back_hbm, map_c.at[pl.ds(rank, LANES)]), (basis_hbm, basis),
                                    (counts_hbm, counts), (kin_hbm, kin_cells), (relax_hbm, relax))):
        consts.append(pltpu.make_async_copy(src, dst, const_sem.at[n]))

    lane = lax.broadcasted_iota(jnp.int32, (1, LANES), 1)
    vy = (((lane // GZ) % GY).astype(jnp.float32) - 0.5 * (GY - 1)) * SPACING
    vz = ((lane % GZ).astype(jnp.float32) - 0.5 * (GZ - 1)) * SPACING
    block = (nz, LANES)
    pos_y = jnp.broadcast_to(vy > 0.0, block)
    pos_z = jnp.broadcast_to(vz > 0.0, block)
    half_y = jnp.broadcast_to(jnp.where(vy > 0.0, 0.5, -0.5), block)
    half_z = jnp.broadcast_to(jnp.where(vz > 0.0, 0.5, -0.5), block)
    rate_y = jnp.broadcast_to(COURANT * jnp.abs(vy), block)
    rate_z = jnp.broadcast_to(COURANT * jnp.abs(vz), block)

    def pick(positive, negative):
        return bit * positive + (1 - bit) * negative

    def across(value, emit, first, last):
        def y_state(mid, before, after):
            return mid + half_y * limited(before, after)

        f = {y: value(y) for y in range(first - 2, first + 2)}
        d = {y: f[y + 1] - f[y] for y in range(first - 2, first + 1)}
        cy = {y: y_state(f[y], d[y - 1], d[y]) for y in (first - 1, first)}
        for y in range(first, last):
            f[y + 2] = value(y + 2)
            d[y + 1] = f[y + 2] - f[y + 1]
            cy[y + 1] = y_state(f[y + 1], d[y], d[y + 1])
            mid = f[y]
            total = rate_y * (cy[y] - jnp.where(pos_y, cy[y - 1], cy[y + 1]))
            dz = pltpu.roll(mid, nz - 1, 0) - mid
            cz = mid + half_z * limited(pltpu.roll(dz, 1, 0), dz)
            total += rate_z * (cz - jnp.where(pos_z, pltpu.roll(cz, 1, 0), pltpu.roll(cz, nz - 1, 0)))
            emit(y, mid, total)

    def speed(tile):
        return COURANT * jnp.abs((tile.astype(jnp.float32) - 0.5 * (GX - 1)) * SPACING)

    def transport(dest, h):
        def row(y):
            return lax.rem(h * hy + y + ny, ny) * nz

        @pl.loop(0, tiles)
        def _(t):
            cols = pl.ds(pl.multiple_of(t * LANES, LANES), LANES)
            rate_x = speed(lax.div(me * width + t * LANES, GY * GZ))
            for j in range(ppd):
                index = 2 + dest * ppd + pick(j, ppd - 1 - j)

                def at(k, y):
                    return cur[pl.ds(pl.multiple_of(k * plane + row(y), nz), nz), cols]

                def emit(y, mid, total):
                    down, up = at(index + sign, y), at(index - sign, y)
                    cx = state(up, mid, down)
                    keep = pl.ds(y * nz, nz)
                    if j == 0:
                        before = state(at(index - 2 * sign, y), up, mid)
                    else:
                        before = cprev[keep]
                    if j < ppd - 1:
                        cprev[keep] = cx
                    result = mid - (total + rate_x * (cx - before))
                    sendbuf[index - 2, pl.ds(pl.multiple_of(row(y), nz), nz), cols] = result.astype(jnp.bfloat16)

                across(lambda y: at(index, y), emit, 0, hy)

    def own_lanes(v):
        return pl.ds(pl.multiple_of(v * width, width), width)

    def row_src(dest, h):
        return sendbuf.at[pl.ds(dest * ppd, ppd), pl.ds(pl.multiple_of(h * half, half), half)]

    def row_copy(dest, peer, r, h):
        return pltpu.make_async_remote_copy(
            src_ref=row_src(dest, h), dst_ref=recv.at[h, :, :, own_lanes(me)],
            send_sem=row_send.at[h, r], recv_sem=row_recv.at[h, r],
            device_id={"vel": peer}, device_id_type=MESH)

    def row_local(h):
        return pltpu.make_async_copy(row_src(mine, h), recv.at[h, :, :, own_lanes(me)], local_sem.at[0, h])

    def unit(dest, h):
        transport(dest, h)
        send(dest, h)

    def send(dest, h):
        peer = vel_of(slab, dest)
        r = lax.rem(peer - me + groups, groups)

        @pl.when(r == 0)
        def _():
            row_local(h).start()

        @pl.when(r != 0)
        def _():
            row_copy(dest, peer, r, h).start()

    edge = 2 if ppd == 1 else 1
    mid_count = groups - 2 * edge
    far_count = groups - 4 * edge

    def mid_dest(k):
        return edge + lax.rem(mine + k, mid_count)

    def edge_dest(k):
        n = lax.rem(mine + k, 2 * edge)
        return n + lax.div(n, edge) * mid_count

    def near_dest(k):
        n = lax.rem(mine + k, 2 * edge)
        return edge + n + lax.div(n, edge) * far_count

    def far_dest(k):
        return 2 * edge + lax.rem(mine + k, far_count)

    def row_list(h):
        out = []
        for r in range(1, groups):
            peer = lax.rem(me + r, groups)
            out.append(row_copy(chain_of(slab, peer), peer, r, h))
        return out

    def z_copies(h):
        here = pl.ds(h * half, half)
        return [
            pltpu.make_async_remote_copy(
                src_ref=zsend.at[pl.ds(0, 2), here], dst_ref=zrecv.at[pl.ds(0, 2), here],
                send_sem=z_send.at[h, 0], recv_sem=z_recv.at[h, 0], device_id={"space": ahead}, device_id_type=MESH),
            pltpu.make_async_remote_copy(
                src_ref=zsend.at[pl.ds(2, 1), here], dst_ref=zrecv.at[pl.ds(2, 1), here],
                send_sem=z_send.at[h, 1], recv_sem=z_recv.at[h, 1], device_id={"space": behind}, device_id_type=MESH),
        ]

    def z_place(h):
        for copy in z_list[h]:
            copy.wait_recv()
        for n, at in enumerate((pick(0, nx + 2), pick(1, nx + 3), pick(nx + 2, 1))):
            here = pl.ds(pl.multiple_of(at * plane + h * half, half), half)
            cur[here] = zrecv[n, h * half:(h + 1) * half].astype(jnp.float32)

    def prepare():
        own = ppd * plane
        span = 4 * LANES
        base = mine * (own // LANES)
        eye = lax.broadcasted_iota(jnp.int32, (nz, nz), 0) == lax.broadcasted_iota(jnp.int32, (nz, nz), 1)
        columns = {}
        for j in range(ppd):
            sheet = relax[mine * ppd + j]
            for h in range(HALVES):
                parts = []
                for y in range(hy):
                    line = jnp.broadcast_to(sheet[h * hy + y:h * hy + y + 1, :], (nz, nz))
                    one = jnp.sum(jnp.where(eye, line, 0.0), axis=1, keepdims=True)
                    parts.append(jnp.broadcast_to(one, (nz, LANES)))
                columns[h, j] = jnp.concatenate(parts, axis=0)
        for step in range(STEPS):
            count = counts[step, slab]
            flags = jnp.zeros((16, LANES), jnp.float32)
            for n in range(cells // span):
                which = kin_cells[step:step + 1, n * span:(n + 1) * span]
                live = n * span + lax.broadcasted_iota(jnp.int32, (1, span), 1) < count
                quotient = jnp.where(live, lax.div(which, LANES) - base, -1)
                hot_high = lax.broadcasted_iota(jnp.int32, (16, span), 0) == quotient
                hot_low = lax.broadcasted_iota(jnp.int32, (LANES, span), 0) == lax.rem(which, LANES)
                flags += lax.dot_general(
                    jnp.where(hot_high, 1.0, 0.0).astype(jnp.bfloat16), jnp.where(hot_low, 1.0, 0.0).astype(jnp.bfloat16),
                    (((1,), (1,)), ((), ())), preferred_element_type=jnp.float32)
            for j in range(ppd):
                for h in range(HALVES):
                    n = j * HALVES + h
                    kin = jnp.broadcast_to(flags[n:n + 1], (LANES, LANES)).T > 0.5
                    rate = columns[h, j]
                    here = pl.ds(j * half, half)
                    coef[step, 0, h, here] = jnp.where(kin, 1.0, 1.0 - rate)
                    coef[step, 1, h, here] = jnp.where(kin, COLLIDE, rate)
                    coef[step, 2, h, here] = jnp.where(kin, 1.0, 0.0)

    def wide(x):
        return jnp.concatenate([x] * (TILE // LANES), axis=1)

    def collide(step, h):
        rows = recv.at[h]

        def lhs():
            return rows[...].reshape(block_rows, nv)

        @pl.loop(0, rank // TILE)
        def _(n):
            cols = pl.ds(pl.multiple_of(n * TILE, TILE), TILE)
            first = jnp.dot(lhs(), map_a[:, cols], preferred_element_type=jnp.float32)
            second = jnp.dot(lhs(), map_b[:, cols], preferred_element_type=jnp.float32)
            hid[:, cols] = (first * second * wide(coef[step, 2, h])).astype(jnp.bfloat16)

        mom = jnp.dot(lhs(), basis[...], preferred_element_type=jnp.float32)
        high = mom.astype(jnp.bfloat16).astype(jnp.float32)
        is_low = (lax.broadcasted_iota(jnp.int32, mom.shape, 1) // 8) == 1
        split = jnp.where(is_low, mom - high, high)
        hid[:, rank:rank + LANES] = (split * (1.0 - coef[step, 2, h])).astype(jnp.bfloat16)

        @pl.loop(0, nv // TILE)
        def _(n):
            cols = pl.ds(pl.multiple_of(n * TILE, TILE), TILE)
            out = jnp.dot(hid[...], map_c[:, cols], preferred_element_type=jnp.float32)
            for j in range(ppd):
                part = slice(j * half, (j + 1) * half)
                here = pl.ds(h * half, half)
                if step == 0:
                    old = rows[j, :, cols].astype(jnp.float32)
                else:
                    old = mv[j, here, cols]
                new = wide(coef[step, 0, h, part]) * old + wide(coef[step, 1, h, part]) * out[part]
                if step == 0:
                    fown[j, here, cols] = new
                    fsend[h, j, :, cols] = new.astype(jnp.bfloat16)
                else:
                    outbuf[h, j, :, cols] = new.astype(jnp.bfloat16)

    low, high_part = pl.ds(0, nv // 2), pl.ds(nv // 2, nv // 2)
    whole = pl.ds(0, nv)

    def halo_copies(h):
        out = []
        for k, (j, r, lanes) in enumerate((
                (reach * ppd - 2, reach, high_part), (ppd - 1, 1, whole), (0, -1, whole), (ppd + 1 - reach * ppd, -reach, low))):
            out.append(pltpu.make_async_remote_copy(
                src_ref=fsend.at[h, j, :, lanes], dst_ref=halo.at[h, k, :, lanes],
                send_sem=halo_send.at[h, k], recv_sem=halo_recv.at[h, k],
                device_id=along(r), device_id_type=MESH))
        return out

    def sideways(h, spans):
        @pl.loop(0, nv // LANES)
        def _(t):
            cols = pl.ds(pl.multiple_of(t * LANES, LANES), LANES)
            for j in range(ppd):
                def emit(y, mid, total):
                    mv[j, pl.ds((h * hy + y) * nz, nz), cols] = mid - total

                for first, last in spans:
                    across(lambda y: fown[j, pl.ds(((h * hy + y) % ny) * nz, nz), cols], emit, first, last)

    def forward(h):
        half_tiles = nv // LANES // 2
        for up in (-1, 1):
            @pl.loop(0, half_tiles)
            def _(n):
                t = n + (half_tiles if up > 0 else 0)
                cols = pl.ds(pl.multiple_of(t * LANES, LANES), LANES)
                rate_x = speed(t)

                def value(k, y):
                    here = pl.ds(y * nz, nz)
                    if 0 <= k < ppd:
                        return fown[k, pl.ds((h * hy + y) * nz, nz), cols]
                    slot = k + 2 if k < 0 else k - ppd + 2
                    return halo[h, slot, here, cols].astype(jnp.float32)

                order = list(range(ppd)) if up > 0 else list(range(ppd - 1, -1, -1))
                for y in range(hy):
                    line = [order[0] - 2 * up, order[0] - up] + order + [order[-1] + up]
                    f = [value(k, y) for k in line]
                    c = [state(f[n], f[n + 1], f[n + 2]) for n in range(ppd + 1)]
                    here = pl.ds((h * hy + y) * nz, nz)
                    for n, j in enumerate(order):
                        result = mv[j, here, cols] - rate_x * (c[n + 1] - c[n])
                        mv[j, here, cols] = result
                        recv[h, j, pl.ds(y * nz, nz), cols] = result.astype(jnp.bfloat16)

    def res_copies(h):
        out = []
        for r in range(1, groups):
            peer = lax.rem(me + r, groups)
            out.append(pltpu.make_async_remote_copy(
                src_ref=outbuf.at[h, :, :, own_lanes(peer)],
                dst_ref=ret_out.at[pl.ds(mine * ppd, ppd), pl.ds(h * half, half)],
                send_sem=res_send.at[h, r], recv_sem=res_recv.at[h, r],
                device_id={"vel": peer}, device_id_type=MESH))
        return out

    def res_local(h):
        return pltpu.make_async_copy(
            outbuf.at[h, :, :, own_lanes(me)],
            ret_out.at[pl.ds(mine * ppd, ppd), pl.ds(h * half, half)], local_sem.at[1, h])

    for copy in loads[:2]:
        copy.wait()
    for n, at in enumerate((pick(nx, 2), pick(nx + 1, 3), pick(2, nx + 1))):
        zsend[n] = cur[pl.ds(pl.multiple_of(at * plane, plane), plane)].astype(jnp.bfloat16)
    z_list = [z_copies(h) for h in range(HALVES)]
    for copy in loads[2:]:
        copy.wait()
    transport(mid_dest(0), 0)
    pl.semaphore_wait(barrier, groups + 1 + 2 * reach)
    for copy in z_list[0] + z_list[1]:
        copy.start()
    send(mid_dest(0), 0)
    for copy in consts:
        copy.start()

    @pl.loop(1, mid_count + 2 * edge)
    def _(k):
        h = lax.div(k, mid_count)
        unit((1 - h) * mid_dest(k) + h * near_dest(k), h)

    for copy in consts[5:]:
        copy.wait()
    prepare()
    z_place(0)

    @pl.loop(0, 2 * edge + far_count)
    def _(k):
        h = jnp.where(k < 2 * edge, 0, 1)
        unit((1 - h) * edge_dest(k) + h * far_dest(k), h)

    z_place(1)

    @pl.loop(0, 2 * edge)
    def _(k):
        unit(edge_dest(k), 1)

    for copy in consts[:5]:
        copy.wait()
    rows_in = [row_list(h) for h in range(HALVES)]
    halos = [halo_copies(h) for h in range(HALVES)]
    results = [res_copies(h) for h in range(HALVES)]
    inner, outer = [(2, hy - 2)], [(0, 2), (hy - 2, hy)]
    for h in range(HALVES):
        for copy in rows_in[h]:
            copy.wait_recv()
        row_local(h).wait()
        collide(0, h)
        for copy in halos[h]:
            copy.start()
        if h < HALVES - 1:
            sideways(h, inner)
    for h in range(HALVES):
        sideways(h, outer if h < HALVES - 1 else [(0, hy)])
        for copy in halos[h]:
            copy.wait_recv()
        forward(h)
        collide(1, h)
        for copy in results[h]:
            copy.start()
        res_local(h).start()
    for h in range(HALVES):
        for copy in z_list[h] + rows_in[h] + halos[h]:
            copy.wait_send()
        for copy in results[h]:
            copy.wait()
        res_local(h).wait()


def body(dist, relax_rate, kinetic_cells, kinetic_count, map_a, map_b, map_c):
    nx, ny, nz, width = dist.shape
    groups = lax.axis_size("vel")
    slabs = lax.axis_size("space")
    cells = nx * ny * nz
    plane = ny * nz
    nv = groups * width
    rank = map_a.shape[1]
    ppd = nx // groups
    half = plane // HALVES
    basis, back = tables()

    any_space = pl.BlockSpec(memory_space=pl.ANY)
    f32, bf16 = jnp.float32, jnp.bfloat16
    dims = (nx, ny, nz, width, groups, slabs)
    vmem = pl.BlockSpec(memory_space=pltpu.VMEM)
    dma = pltpu.SemaphoreType.DMA
    ret = pl.pallas_call(
        functools.partial(kernel, dims),
        out_shape=pltpu.VMEM((nx, plane, width), bf16),
        in_specs=[any_space] * 9,
        out_specs=vmem,
        scratch_shapes=[
            pltpu.VMEM(((nx + 4) * plane, width), f32),
            pltpu.VMEM((half, LANES), f32),
            pltpu.VMEM((nx, plane, width), bf16),
            pltpu.VMEM((3, plane, width), bf16),
            pltpu.VMEM((3, plane, width), bf16),
            pltpu.VMEM((HALVES, ppd, half, nv), bf16),
            pltpu.VMEM((ppd, plane, nv), f32),
            pltpu.VMEM((HALVES, ppd, half, nv), bf16),
            pltpu.VMEM((HALVES, 4, half, nv), bf16),
            pltpu.VMEM((ppd, plane, nv), f32),
            pltpu.VMEM((HALVES, ppd, half, nv), bf16),
            pltpu.VMEM(map_a.shape, bf16),
            pltpu.VMEM(map_b.shape, bf16),
            pltpu.VMEM((rank + LANES, nv), bf16),
            pltpu.VMEM((nv, LANES), bf16),
            pltpu.VMEM((ppd * half, rank + LANES), bf16),
            pltpu.VMEM((STEPS, 3, HALVES, ppd * half, LANES), f32),
            pltpu.SMEM(kinetic_count.shape, jnp.int32),
            pltpu.VMEM(kinetic_cells.shape, jnp.int32),
            pltpu.VMEM(relax_rate.shape, f32),
            dma((4,)),
            dma((8,)),
            dma((2, HALVES)),
            dma((HALVES, 2)),
            dma((HALVES, 2)),
            dma((HALVES, groups)),
            dma((HALVES, groups)),
            dma((HALVES, 4)),
            dma((HALVES, 4)),
            dma((HALVES, groups)),
            dma((HALVES, groups)),
        ],
        compiler_params=pltpu.CompilerParams(
            collective_id=0, has_side_effects=True, vmem_limit_bytes=64880640),
    )(kinetic_count, kinetic_cells, relax_rate, dist.reshape(cells, width), map_a, map_b, map_c,
      jnp.asarray(basis), jnp.asarray(back))
    parts = 16
    out = pl.pallas_call(
        widen,
        out_shape=jax.ShapeDtypeStruct((cells, width), f32),
        in_specs=[vmem],
        out_specs=any_space,
        scratch_shapes=[
            pltpu.VMEM((parts, cells // parts, width), f32),
            dma((parts,)),
        ],
        compiler_params=pltpu.CompilerParams(vmem_limit_bytes=16 << 20),
    )(ret.reshape(cells, width))
    return out.reshape(dist.shape)


def widen(src, out, wide_buf, out_sem):
    parts = out_sem.shape[0]
    size = src.shape[0] // parts
    outs = [pltpu.make_async_copy(wide_buf.at[n], out.at[pl.ds(n * size, size)], out_sem.at[n]) for n in range(parts)]
    for n in range(parts):
        wide_buf[n] = src[n * size:(n + 1) * size].astype(jnp.float32)
        outs[n].start()
    for copy in outs:
        copy.wait()


def solution(mesh):
    return jax.shard_map(
        body,
        mesh=mesh,
        in_specs=(
            P("space", None, None, "vel"),
            P("space", None, None),
            P(None, "space"),
            P(),
            P(),
            P(),
            P(),
        ),
        out_specs=P("space", None, None, "vel"),
        check_vma=False,
    )
```

```python
import functools

import jax
import jax.numpy as jnp
import numpy as np
from jax import lax
from jax.experimental import pallas as pl
from jax.experimental.pallas import tpu as pltpu
from jax.sharding import PartitionSpec as P

GX = 16
GY = 16
GZ = 8
STEPS = 2
COURANT = 0.1
SPACING = 0.5
COLLIDE = 0.5
LANES = 128
TILE = 256
HALVES = 2
MESH = pl.DeviceIdType.MESH


def tables():
    k = np.arange(GX * GY * GZ)
    vx = ((k // (GY * GZ)) - 0.5 * (GX - 1)) * SPACING
    vy = (((k // GZ) % GY) - 0.5 * (GY - 1)) * SPACING
    vz = ((k % GZ) - 0.5 * (GZ - 1)) * SPACING
    s = vx * vx + vy * vy + vz * vz
    w = np.exp(-0.5 * s)
    w = w / w.sum()
    m2, m4 = (w * s).sum(), (w * s * s).sum()
    kappa = m4 - m2 * m2
    per_e = w * (s - m2) / kappa
    rows = np.stack([
        w - m2 * per_e,
        w * vx / (w * vx * vx).sum(),
        w * vy / (w * vy * vy).sum(),
        w * vz / (w * vz * vz).sum(),
        per_e,
        per_e,
    ])
    s_hi = np.asarray(np.asarray(s, np.float32).astype(jnp.bfloat16), np.float64)
    cols = np.stack([np.ones_like(vx), vx, vy, vz, s_hi, s - s_hi], axis=1)
    g_hi = np.asarray(np.asarray(rows, np.float32).astype(jnp.bfloat16), np.float64)
    g_lo = rows - g_hi
    basis = np.zeros((k.size, LANES))
    back = np.zeros((LANES, k.size))
    for at, part in ((0, g_hi), (8, g_hi), (16, g_lo)):
        basis[:, at:at + 6] = cols
        back[at:at + 6] = part
    return basis.astype(np.float32).astype(jnp.bfloat16), back.astype(np.float32).astype(jnp.bfloat16)


def limited(a, b):
    return jnp.minimum(jnp.maximum(a, jnp.minimum(b, 0.0)), jnp.maximum(b, 0.0))


def state(up, mid, down):
    return mid + 0.5 * limited(mid - up, down - mid)


def kernel(dims, counts_hbm, kin_hbm, relax_hbm, dist, a_hbm, b_hbm, c_hbm, basis_hbm, back_hbm,
           wide_out,
           cur, cprev, sendbuf, zsend, zrecv, recv, fown, fsend, halo, mv, outbuf,
           map_a, map_b, map_c, basis, hid, coef, counts, kin_cells, relax, ret_out,
           load_sem, const_sem, local_sem, z_send, z_recv, row_send, row_recv, halo_send, halo_recv, res_send, res_recv):
    nx, ny, nz, width, groups, slabs = dims
    plane = ny * nz
    cells = nx * plane
    nv = groups * width
    rank = map_a.shape[1]
    ppd = nx // groups
    hy = ny // HALVES
    half = hy * nz
    block_rows = ppd * half
    tiles = width // LANES
    nchips = groups // 2
    ncol = groups // 4
    me = lax.axis_index("vel")
    slab = lax.axis_index("space")
    first_x = lax.div(me * width, GY * GZ)
    bit = lax.div(first_x, GX // 2)
    sign = 2 * bit - 1
    ahead = lax.rem(slab + sign + slabs, slabs)
    behind = lax.rem(slab - sign + slabs, slabs)

    def vel_of(s, p):
        q = lax.rem(lax.div(p, 2) + nchips * slabs - s, nchips)
        y = lax.div(q, ncol)
        x = lax.rem(q, ncol)
        return (y * ncol + x + y * (ncol - 1 - 2 * x)) * 2 + lax.rem(p, 2)

    def chain_of(s, v):
        chip = lax.div(v, 2)
        y = lax.div(chip, ncol)
        x = lax.rem(chip, ncol)
        q = y * ncol + x + y * (ncol - 1 - 2 * x)
        return 2 * lax.rem(q + s, nchips) + lax.rem(v, 2)

    mine = chain_of(slab, me)

    def along(r):
        at = mine + r + groups
        s = lax.rem(slab + lax.div(at, groups) - 1 + slabs, slabs)
        return {"space": s, "vel": vel_of(s, lax.rem(at, groups))}

    reach = 1 if ppd > 1 else 2
    barrier = pltpu.get_barrier_semaphore()
    pl.semaphore_signal(barrier, inc=1, device_id={"space": ahead}, device_id_type=MESH)
    pl.semaphore_signal(barrier, inc=1, device_id={"space": behind}, device_id_type=MESH)
    for r in range(1, reach + 1):
        pl.semaphore_signal(barrier, inc=1, device_id=along(r), device_id_type=MESH)
        pl.semaphore_signal(barrier, inc=1, device_id=along(-r), device_id_type=MESH)
    for p in range(1, groups):
        pl.semaphore_signal(barrier, inc=1, device_id={"vel": lax.rem(me + p, groups)}, device_id_type=MESH)

    edge = 2 if ppd == 1 else 1
    mid_count = groups - 2 * edge
    far_count = groups - 4 * edge

    def mid_dest(k):
        return edge + lax.rem(mine + k, mid_count)

    loads = []
    for n in range(groups):
        size = ppd * plane
        at = pl.multiple_of(lax.rem(mid_dest(0) - edge + n, groups) * size, size)
        loads.append(pltpu.make_async_copy(
            dist.at[pl.ds(at, size)], cur.at[pl.ds(2 * plane + at, size)], load_sem.at[n]))
        loads[-1].start()
    consts = []
    for n, (src, dst) in enumerate(((a_hbm, map_a), (b_hbm, map_b), (c_hbm, map_c.at[pl.ds(0, rank)]),
                                    (back_hbm, map_c.at[pl.ds(rank, LANES)]), (basis_hbm, basis),
                                    (counts_hbm, counts), (kin_hbm, kin_cells), (relax_hbm, relax))):
        consts.append(pltpu.make_async_copy(src, dst, const_sem.at[n]))

    lane = lax.broadcasted_iota(jnp.int32, (1, LANES), 1)
    vy = (((lane // GZ) % GY).astype(jnp.float32) - 0.5 * (GY - 1)) * SPACING
    vz = ((lane % GZ).astype(jnp.float32) - 0.5 * (GZ - 1)) * SPACING
    block = (nz, LANES)
    pos_y = jnp.broadcast_to(vy > 0.0, block)
    pos_z = jnp.broadcast_to(vz > 0.0, block)
    half_y = jnp.broadcast_to(jnp.where(vy > 0.0, 0.5, -0.5), block)
    half_z = jnp.broadcast_to(jnp.where(vz > 0.0, 0.5, -0.5), block)
    rate_y = jnp.broadcast_to(COURANT * jnp.abs(vy), block)
    rate_z = jnp.broadcast_to(COURANT * jnp.abs(vz), block)

    def pick(positive, negative):
        return bit * positive + (1 - bit) * negative

    def across(value, emit, first, last):
        def y_state(mid, before, after):
            return mid + half_y * limited(before, after)

        f = {y: value(y) for y in range(first - 2, first + 2)}
        d = {y: f[y + 1] - f[y] for y in range(first - 2, first + 1)}
        cy = {y: y_state(f[y], d[y - 1], d[y]) for y in (first - 1, first)}
        for y in range(first, last):
            f[y + 2] = value(y + 2)
            d[y + 1] = f[y + 2] - f[y + 1]
            cy[y + 1] = y_state(f[y + 1], d[y], d[y + 1])
            mid = f[y]
            total = rate_y * (cy[y] - jnp.where(pos_y, cy[y - 1], cy[y + 1]))
            dz = pltpu.roll(mid, nz - 1, 0) - mid
            cz = mid + half_z * limited(pltpu.roll(dz, 1, 0), dz)
            total += rate_z * (cz - jnp.where(pos_z, pltpu.roll(cz, 1, 0), pltpu.roll(cz, nz - 1, 0)))
            emit(y, mid, total)

    def speed(tile):
        return COURANT * jnp.abs((tile.astype(jnp.float32) - 0.5 * (GX - 1)) * SPACING)

    def transport(dest, h):
        def row(y):
            return lax.rem(h * hy + y + ny, ny) * nz

        @pl.loop(0, tiles)
        def _(t):
            cols = pl.ds(pl.multiple_of(t * LANES, LANES), LANES)
            rate_x = speed(lax.div(me * width + t * LANES, GY * GZ))
            for j in range(ppd):
                index = 2 + dest * ppd + pick(j, ppd - 1 - j)

                def at(k, y):
                    return cur[pl.ds(pl.multiple_of(k * plane + row(y), nz), nz), cols]

                def emit(y, mid, total):
                    down, up = at(index + sign, y), at(index - sign, y)
                    cx = state(up, mid, down)
                    keep = pl.ds(y * nz, nz)
                    if j == 0:
                        before = state(at(index - 2 * sign, y), up, mid)
                    else:
                        before = cprev[keep]
                    if j < ppd - 1:
                        cprev[keep] = cx
                    result = mid - (total + rate_x * (cx - before))
                    sendbuf[index - 2, pl.ds(pl.multiple_of(row(y), nz), nz), cols] = result.astype(jnp.bfloat16)

                across(lambda y: at(index, y), emit, 0, hy)

    def own_lanes(v):
        return pl.ds(pl.multiple_of(v * width, width), width)

    def row_src(dest, h):
        return sendbuf.at[pl.ds(dest * ppd, ppd), pl.ds(pl.multiple_of(h * half, half), half)]

    def row_copy(dest, peer, r, h):
        return pltpu.make_async_remote_copy(
            src_ref=row_src(dest, h), dst_ref=recv.at[h, :, :, own_lanes(me)],
            send_sem=row_send.at[h, r], recv_sem=row_recv.at[h, r],
            device_id={"vel": peer}, device_id_type=MESH)

    def row_local(h):
        return pltpu.make_async_copy(row_src(mine, h), recv.at[h, :, :, own_lanes(me)], local_sem.at[0, h])

    def unit(dest, h):
        transport(dest, h)
        send(dest, h)

    def send(dest, h):
        peer = vel_of(slab, dest)
        r = lax.rem(peer - me + groups, groups)

        @pl.when(r == 0)
        def _():
            row_local(h).start()

        @pl.when(r != 0)
        def _():
            row_copy(dest, peer, r, h).start()

    def edge_dest(k):
        n = lax.rem(mine + k, 2 * edge)
        return n + lax.div(n, edge) * mid_count

    def near_dest(k):
        n = lax.rem(mine + k, 2 * edge)
        return edge + n + lax.div(n, edge) * far_count

    def far_dest(k):
        return 2 * edge + lax.rem(mine + k, far_count)

    def row_list(h):
        out = []
        for r in range(1, groups):
            peer = lax.rem(me + r, groups)
            out.append(row_copy(chain_of(slab, peer), peer, r, h))
        return out

    def z_copies(h):
        here = pl.ds(h * half, half)
        return [
            pltpu.make_async_remote_copy(
                src_ref=zsend.at[pl.ds(0, 2), here], dst_ref=zrecv.at[pl.ds(0, 2), here],
                send_sem=z_send.at[h, 0], recv_sem=z_recv.at[h, 0], device_id={"space": ahead}, device_id_type=MESH),
            pltpu.make_async_remote_copy(
                src_ref=zsend.at[pl.ds(2, 1), here], dst_ref=zrecv.at[pl.ds(2, 1), here],
                send_sem=z_send.at[h, 1], recv_sem=z_recv.at[h, 1], device_id={"space": behind}, device_id_type=MESH),
        ]

    def z_place(h):
        for copy in z_list[h]:
            copy.wait_recv()
        for n, at in enumerate((pick(0, nx + 2), pick(1, nx + 3), pick(nx + 2, 1))):
            here = pl.ds(pl.multiple_of(at * plane + h * half, half), half)
            cur[here] = zrecv[n, h * half:(h + 1) * half].astype(jnp.float32)

    def prepare():
        own = ppd * plane
        span = 4 * LANES
        base = mine * (own // LANES)
        eye = lax.broadcasted_iota(jnp.int32, (nz, nz), 0) == lax.broadcasted_iota(jnp.int32, (nz, nz), 1)
        columns = {}
        for j in range(ppd):
            sheet = relax[mine * ppd + j]
            for h in range(HALVES):
                parts = []
                for y in range(hy):
                    line = jnp.broadcast_to(sheet[h * hy + y:h * hy + y + 1, :], (nz, nz))
                    one = jnp.sum(jnp.where(eye, line, 0.0), axis=1, keepdims=True)
                    parts.append(jnp.broadcast_to(one, (nz, LANES)))
                columns[h, j] = jnp.concatenate(parts, axis=0)
        for step in range(STEPS):
            count = counts[step, slab]
            flags = jnp.zeros((16, LANES), jnp.float32)
            for n in range(cells // span):
                which = kin_cells[step:step + 1, n * span:(n + 1) * span]
                live = n * span + lax.broadcasted_iota(jnp.int32, (1, span), 1) < count
                quotient = jnp.where(live, lax.div(which, LANES) - base, -1)
                hot_high = lax.broadcasted_iota(jnp.int32, (16, span), 0) == quotient
                hot_low = lax.broadcasted_iota(jnp.int32, (LANES, span), 0) == lax.rem(which, LANES)
                flags += lax.dot_general(
                    jnp.where(hot_high, 1.0, 0.0).astype(jnp.bfloat16), jnp.where(hot_low, 1.0, 0.0).astype(jnp.bfloat16),
                    (((1,), (1,)), ((), ())), preferred_element_type=jnp.float32)
            for j in range(ppd):
                for h in range(HALVES):
                    n = j * HALVES + h
                    kin = jnp.broadcast_to(flags[n:n + 1], (LANES, LANES)).T > 0.5
                    rate = columns[h, j]
                    here = pl.ds(j * half, half)
                    coef[step, 0, h, here] = jnp.where(kin, 1.0, 1.0 - rate)
                    coef[step, 1, h, here] = jnp.where(kin, COLLIDE, rate)
                    coef[step, 2, h, here] = jnp.where(kin, 1.0, 0.0)

    def wide(x):
        return jnp.concatenate([x] * (TILE // LANES), axis=1)

    def collide(step, h):
        rows = recv.at[h]

        def lhs():
            return rows[...].reshape(block_rows, nv)

        @pl.loop(0, rank // TILE, unroll=True)
        def _(n):
            cols = pl.ds(pl.multiple_of(n * TILE, TILE), TILE)
            first = jnp.dot(lhs(), map_a[:, cols], preferred_element_type=jnp.float32)
            second = jnp.dot(lhs(), map_b[:, cols], preferred_element_type=jnp.float32)
            hid[:, cols] = (first * second * wide(coef[step, 2, h])).astype(jnp.bfloat16)

        mom = jnp.dot(lhs(), basis[...], preferred_element_type=jnp.float32)
        high = mom.astype(jnp.bfloat16).astype(jnp.float32)
        is_low = (lax.broadcasted_iota(jnp.int32, mom.shape, 1) // 8) == 1
        split = jnp.where(is_low, mom - high, high)
        hid[:, rank:rank + LANES] = (split * (1.0 - coef[step, 2, h])).astype(jnp.bfloat16)

        @pl.loop(0, nv // TILE)
        def _(n):
            cols = pl.ds(pl.multiple_of(n * TILE, TILE), TILE)
            out = jnp.dot(hid[...], map_c[:, cols], preferred_element_type=jnp.float32)
            for j in range(ppd):
                part = slice(j * half, (j + 1) * half)
                here = pl.ds(h * half, half)
                if step == 0:
                    old = rows[j, :, cols].astype(jnp.float32)
                else:
                    old = mv[j, here, cols]
                new = wide(coef[step, 0, h, part]) * old + wide(coef[step, 1, h, part]) * out[part]
                if step == 0:
                    fown[j, here, cols] = new
                    fsend[h, j, :, cols] = new.astype(jnp.bfloat16)
                else:
                    outbuf[h, j, :, cols] = new.astype(jnp.bfloat16)

    low, high_part = pl.ds(0, nv // 2), pl.ds(nv // 2, nv // 2)
    whole = pl.ds(0, nv)

    def halo_copies(h):
        out = []
        for k, (j, r, lanes) in enumerate((
                (reach * ppd - 2, reach, high_part), (ppd - 1, 1, whole), (0, -1, whole), (ppd + 1 - reach * ppd, -reach, low))):
            out.append(pltpu.make_async_remote_copy(
                src_ref=fsend.at[h, j, :, lanes], dst_ref=halo.at[h, k, :, lanes],
                send_sem=halo_send.at[h, k], recv_sem=halo_recv.at[h, k],
                device_id=along(r), device_id_type=MESH))
        return out

    def sideways(h, spans):
        @pl.loop(0, nv // LANES)
        def _(t):
            cols = pl.ds(pl.multiple_of(t * LANES, LANES), LANES)
            for j in range(ppd):
                def emit(y, mid, total):
                    mv[j, pl.ds((h * hy + y) * nz, nz), cols] = mid - total

                for first, last in spans:
                    across(lambda y: fown[j, pl.ds(((h * hy + y) % ny) * nz, nz), cols], emit, first, last)

    def forward(h):
        half_tiles = nv // LANES // 2
        for up in (-1, 1):
            @pl.loop(0, half_tiles)
            def _(n):
                t = n + (half_tiles if up > 0 else 0)
                cols = pl.ds(pl.multiple_of(t * LANES, LANES), LANES)
                rate_x = speed(t)

                def value(k, y):
                    here = pl.ds(y * nz, nz)
                    if 0 <= k < ppd:
                        return fown[k, pl.ds((h * hy + y) * nz, nz), cols]
                    slot = k + 2 if k < 0 else k - ppd + 2
                    return halo[h, slot, here, cols].astype(jnp.float32)

                order = list(range(ppd)) if up > 0 else list(range(ppd - 1, -1, -1))
                for y in range(hy):
                    line = [order[0] - 2 * up, order[0] - up] + order + [order[-1] + up]
                    f = [value(k, y) for k in line]
                    c = [state(f[n], f[n + 1], f[n + 2]) for n in range(ppd + 1)]
                    here = pl.ds((h * hy + y) * nz, nz)
                    for n, j in enumerate(order):
                        result = mv[j, here, cols] - rate_x * (c[n + 1] - c[n])
                        mv[j, here, cols] = result
                        recv[h, j, pl.ds(y * nz, nz), cols] = result.astype(jnp.bfloat16)

    def res_copies(h):
        out = []
        for r in range(1, groups):
            peer = lax.rem(me + r, groups)
            out.append(pltpu.make_async_remote_copy(
                src_ref=outbuf.at[h, :, :, own_lanes(peer)],
                dst_ref=ret_out.at[pl.ds(mine * ppd, ppd), pl.ds(h * half, half)],
                send_sem=res_send.at[h, r], recv_sem=res_recv.at[h, r],
                device_id={"vel": peer}, device_id_type=MESH))
        return out

    def res_local(h):
        return pltpu.make_async_copy(
            outbuf.at[h, :, :, own_lanes(me)],
            ret_out.at[pl.ds(mine * ppd, ppd), pl.ds(h * half, half)], local_sem.at[1, h])

    def widen(at, h):
        here = (pl.ds(at * ppd, ppd), pl.ds(h * half, half))
        wide_out[here] = ret_out[here].astype(jnp.float32)

    for copy in loads[:2 * edge + 1]:
        copy.wait()
    transport(mid_dest(0), 0)
    pl.semaphore_wait(barrier, groups + 1 + 2 * reach)
    send(mid_dest(0), 0)
    for copy in loads[2 * edge + 1:]:
        copy.wait()
    for n, at in enumerate((pick(nx, 2), pick(nx + 1, 3), pick(2, nx + 1))):
        zsend[n] = cur[pl.ds(pl.multiple_of(at * plane, plane), plane)].astype(jnp.bfloat16)
    z_list = [z_copies(h) for h in range(HALVES)]
    for copy in z_list[0] + z_list[1]:
        copy.start()
    for copy in consts:
        copy.start()

    @pl.loop(1, mid_count + 2 * edge)
    def _(k):
        h = lax.div(k, mid_count)
        unit((1 - h) * mid_dest(k) + h * near_dest(k), h)

    for copy in consts[5:]:
        copy.wait()
    prepare()
    z_place(0)

    @pl.loop(0, 2 * edge + far_count)
    def _(k):
        h = jnp.where(k < 2 * edge, 0, 1)
        unit((1 - h) * edge_dest(k) + h * far_dest(k), h)

    z_place(1)

    @pl.loop(0, 2 * edge)
    def _(k):
        unit(edge_dest(k), 1)

    for copy in consts[:5]:
        copy.wait()
    rows_in = [row_list(h) for h in range(HALVES)]
    halos = [halo_copies(h) for h in range(HALVES)]
    results = [res_copies(h) for h in range(HALVES)]
    inner, outer = [(2, hy - 2)], [(0, 2), (hy - 2, hy)]
    for h in range(HALVES):
        for copy in rows_in[h]:
            copy.wait_recv()
        row_local(h).wait()
        collide(0, h)
        for copy in halos[h]:
            copy.start()
        if h < HALVES - 1:
            sideways(h, inner)
    for h in range(HALVES):
        sideways(h, outer if h < HALVES - 1 else [(0, hy)])
        for copy in halos[h]:
            copy.wait_recv()
        forward(h)
        collide(1, h)
        for copy in results[h]:
            copy.start()
        res_local(h).start()
    for h in range(HALVES):
        for copy in z_list[h] + rows_in[h] + halos[h]:
            copy.wait_send()
        res_local(h).wait()
        widen(mine, h)
        for r, copy in enumerate(results[h], 1):
            copy.wait()
            widen(chain_of(slab, lax.rem(me - r + groups, groups)), h)


def body(dist, relax_rate, kinetic_cells, kinetic_count, map_a, map_b, map_c):
    nx, ny, nz, width = dist.shape
    groups = lax.axis_size("vel")
    slabs = lax.axis_size("space")
    cells = nx * ny * nz
    plane = ny * nz
    nv = groups * width
    rank = map_a.shape[1]
    ppd = nx // groups
    half = plane // HALVES
    basis, back = tables()

    any_space = pl.BlockSpec(memory_space=pl.ANY)
    f32, bf16 = jnp.float32, jnp.bfloat16
    dims = (nx, ny, nz, width, groups, slabs)
    vmem = pl.BlockSpec(memory_space=pltpu.VMEM)
    dma = pltpu.SemaphoreType.DMA
    ret = pl.pallas_call(
        functools.partial(kernel, dims),
        out_shape=pltpu.VMEM((nx, plane, width), f32),
        in_specs=[any_space] * 9,
        out_specs=vmem,
        scratch_shapes=[
            pltpu.VMEM(((nx + 4) * plane, width), f32),
            pltpu.VMEM((half, LANES), f32),
            pltpu.VMEM((nx, plane, width), bf16),
            pltpu.VMEM((3, plane, width), bf16),
            pltpu.VMEM((3, plane, width), bf16),
            pltpu.VMEM((HALVES, ppd, half, nv), bf16),
            pltpu.VMEM((ppd, plane, nv), f32),
            pltpu.VMEM((HALVES, ppd, half, nv), bf16),
            pltpu.VMEM((HALVES, 4, half, nv), bf16),
            pltpu.VMEM((ppd, plane, nv), f32),
            pltpu.VMEM((HALVES, ppd, half, nv), bf16),
            pltpu.VMEM(map_a.shape, bf16),
            pltpu.VMEM(map_b.shape, bf16),
            pltpu.VMEM((rank + LANES, nv), bf16),
            pltpu.VMEM((nv, LANES), bf16),
            pltpu.VMEM((ppd * half, rank + LANES), bf16),
            pltpu.VMEM((STEPS, 3, HALVES, ppd * half, LANES), f32),
            pltpu.SMEM(kinetic_count.shape, jnp.int32),
            pltpu.VMEM(kinetic_cells.shape, jnp.int32),
            pltpu.VMEM(relax_rate.shape, f32),
            pltpu.VMEM((nx, plane, width), bf16),
            dma((groups,)),
            dma((8,)),
            dma((2, HALVES)),
            dma((HALVES, 2)),
            dma((HALVES, 2)),
            dma((HALVES, groups)),
            dma((HALVES, groups)),
            dma((HALVES, 4)),
            dma((HALVES, 4)),
            dma((HALVES, groups)),
            dma((HALVES, groups)),
        ],
        compiler_params=pltpu.CompilerParams(
            collective_id=0, has_side_effects=True, vmem_limit_bytes=62783488),
    )(kinetic_count, kinetic_cells, relax_rate, dist.reshape(cells, width), map_a, map_b, map_c,
      jnp.asarray(basis), jnp.asarray(back))
    return ret.reshape(dist.shape)


def solution(mesh):
    return jax.shard_map(
        body,
        mesh=mesh,
        in_specs=(
            P("space", None, None, "vel"),
            P("space", None, None),
            P(None, "space"),
            P(),
            P(),
            P(),
            P(),
        ),
        out_specs=P("space", None, None, "vel"),
        check_vma=False,
    )
```

```python
import functools

import jax
import jax.numpy as jnp
import numpy as np
from jax import lax
from jax.experimental import pallas as pl
from jax.experimental.pallas import tpu as pltpu
from jax.sharding import PartitionSpec as P

GX = 16
GY = 16
GZ = 8
STEPS = 2
COURANT = 0.1
SPACING = 0.5
COLLIDE = 0.5
LANES = 128
TILE = 256
HALVES = 2
MESH = pl.DeviceIdType.MESH


def tables():
    k = np.arange(GX * GY * GZ)
    vx = ((k // (GY * GZ)) - 0.5 * (GX - 1)) * SPACING
    vy = (((k // GZ) % GY) - 0.5 * (GY - 1)) * SPACING
    vz = ((k % GZ) - 0.5 * (GZ - 1)) * SPACING
    s = vx * vx + vy * vy + vz * vz
    w = np.exp(-0.5 * s)
    w = w / w.sum()
    m2, m4 = (w * s).sum(), (w * s * s).sum()
    kappa = m4 - m2 * m2
    per_e = w * (s - m2) / kappa
    rows = np.stack([
        w - m2 * per_e,
        w * vx / (w * vx * vx).sum(),
        w * vy / (w * vy * vy).sum(),
        w * vz / (w * vz * vz).sum(),
        per_e,
        per_e,
    ])
    s_hi = np.asarray(np.asarray(s, np.float32).astype(jnp.bfloat16), np.float64)
    cols = np.stack([np.ones_like(vx), vx, vy, vz, s_hi, s - s_hi], axis=1)
    g_hi = np.asarray(np.asarray(rows, np.float32).astype(jnp.bfloat16), np.float64)
    g_lo = rows - g_hi
    basis = np.zeros((k.size, LANES))
    back = np.zeros((LANES, k.size))
    for at, part in ((0, g_hi), (8, g_hi), (16, g_lo)):
        basis[:, at:at + 6] = cols
        back[at:at + 6] = part
    return basis.astype(np.float32).astype(jnp.bfloat16), back.astype(np.float32).astype(jnp.bfloat16)


def limited(a, b):
    return jnp.minimum(jnp.maximum(a, jnp.minimum(b, 0.0)), jnp.maximum(b, 0.0))


def state(up, mid, down):
    return mid + 0.5 * limited(mid - up, down - mid)


def kernel(dims, counts_hbm, kin_hbm, relax_hbm, dist, a_hbm, b_hbm, c_hbm, basis_hbm, back_hbm,
           wide_out,
           cur, cprev, sendbuf, zsend, zrecv, recv, fown, fsend, halo, mv, outbuf,
           map_a, map_b, map_c, basis, hid, coef, counts, kin_cells, relax, ret_out,
           load_sem, const_sem, local_sem, z_send, z_recv, row_send, row_recv, halo_send, halo_recv, res_send, res_recv):
    nx, ny, nz, width, groups, slabs = dims
    plane = ny * nz
    cells = nx * plane
    nv = groups * width
    rank = map_a.shape[1]
    ppd = nx // groups
    hy = ny // HALVES
    half = hy * nz
    block_rows = ppd * half
    tiles = width // LANES
    nchips = groups // 2
    ncol = groups // 4
    me = lax.axis_index("vel")
    slab = lax.axis_index("space")
    first_x = lax.div(me * width, GY * GZ)
    bit = lax.div(first_x, GX // 2)
    sign = 2 * bit - 1
    ahead = lax.rem(slab + sign + slabs, slabs)
    behind = lax.rem(slab - sign + slabs, slabs)

    def vel_of(s, p):
        q = lax.rem(lax.div(p, 2) + nchips * slabs - s, nchips)
        y = lax.div(q, ncol)
        x = lax.rem(q, ncol)
        return (y * ncol + x + y * (ncol - 1 - 2 * x)) * 2 + lax.rem(p, 2)

    def chain_of(s, v):
        chip = lax.div(v, 2)
        y = lax.div(chip, ncol)
        x = lax.rem(chip, ncol)
        q = y * ncol + x + y * (ncol - 1 - 2 * x)
        return 2 * lax.rem(q + s, nchips) + lax.rem(v, 2)

    mine = chain_of(slab, me)

    def along(r):
        at = mine + r + groups
        s = lax.rem(slab + lax.div(at, groups) - 1 + slabs, slabs)
        return {"space": s, "vel": vel_of(s, lax.rem(at, groups))}

    reach = 1 if ppd > 1 else 2
    barrier = pltpu.get_barrier_semaphore()
    pl.semaphore_signal(barrier, inc=1, device_id={"space": ahead}, device_id_type=MESH)
    pl.semaphore_signal(barrier, inc=1, device_id={"space": behind}, device_id_type=MESH)
    for r in range(1, reach + 1):
        pl.semaphore_signal(barrier, inc=1, device_id=along(r), device_id_type=MESH)
        pl.semaphore_signal(barrier, inc=1, device_id=along(-r), device_id_type=MESH)
    for p in range(1, groups):
        pl.semaphore_signal(barrier, inc=1, device_id={"vel": lax.rem(me + p, groups)}, device_id_type=MESH)

    edge = 2 if ppd == 1 else 1
    mid_count = groups - 2 * edge
    far_count = groups - 4 * edge

    def mid_dest(k):
        return edge + lax.rem(mine + k + 1, mid_count)

    loads = []
    for n in range(groups):
        size = ppd * plane
        at = pl.multiple_of(lax.rem(mid_dest(0) - edge + n, groups) * size, size)
        loads.append(pltpu.make_async_copy(
            dist.at[pl.ds(at, size)], cur.at[pl.ds(2 * plane + at, size)], load_sem.at[n]))
        loads[-1].start()
    consts = []
    for n, (src, dst) in enumerate(((a_hbm, map_a), (b_hbm, map_b), (c_hbm, map_c.at[pl.ds(0, rank)]),
                                    (back_hbm, map_c.at[pl.ds(rank, LANES)]), (basis_hbm, basis),
                                    (counts_hbm, counts), (kin_hbm, kin_cells), (relax_hbm, relax))):
        consts.append(pltpu.make_async_copy(src, dst, const_sem.at[n]))

    lane = lax.broadcasted_iota(jnp.int32, (1, LANES), 1)
    vy = (((lane // GZ) % GY).astype(jnp.float32) - 0.5 * (GY - 1)) * SPACING
    vz = ((lane % GZ).astype(jnp.float32) - 0.5 * (GZ - 1)) * SPACING
    block = (nz, LANES)
    pos_y = jnp.broadcast_to(vy > 0.0, block)
    pos_z = jnp.broadcast_to(vz > 0.0, block)
    half_y = jnp.broadcast_to(jnp.where(vy > 0.0, 0.5, -0.5), block)
    half_z = jnp.broadcast_to(jnp.where(vz > 0.0, 0.5, -0.5), block)
    rate_y = jnp.broadcast_to(COURANT * jnp.abs(vy), block)
    rate_z = jnp.broadcast_to(COURANT * jnp.abs(vz), block)

    def pick(positive, negative):
        return bit * positive + (1 - bit) * negative

    def across(value, emit, first, last):
        def y_state(mid, before, after):
            return mid + half_y * limited(before, after)

        f = {y: value(y) for y in range(first - 2, first + 2)}
        d = {y: f[y + 1] - f[y] for y in range(first - 2, first + 1)}
        cy = {y: y_state(f[y], d[y - 1], d[y]) for y in (first - 1, first)}
        for y in range(first, last):
            f[y + 2] = value(y + 2)
            d[y + 1] = f[y + 2] - f[y + 1]
            cy[y + 1] = y_state(f[y + 1], d[y], d[y + 1])
            mid = f[y]
            total = rate_y * (cy[y] - jnp.where(pos_y, cy[y - 1], cy[y + 1]))
            dz = pltpu.roll(mid, nz - 1, 0) - mid
            cz = mid + half_z * limited(pltpu.roll(dz, 1, 0), dz)
            total += rate_z * (cz - jnp.where(pos_z, pltpu.roll(cz, 1, 0), pltpu.roll(cz, nz - 1, 0)))
            emit(y, mid, total)

    def speed(tile):
        return COURANT * jnp.abs((tile.astype(jnp.float32) - 0.5 * (GX - 1)) * SPACING)

    def transport(dest, h):
        def row(y):
            return lax.rem(h * hy + y + ny, ny) * nz

        @pl.loop(0, tiles)
        def _(t):
            cols = pl.ds(pl.multiple_of(t * LANES, LANES), LANES)
            rate_x = speed(lax.div(me * width + t * LANES, GY * GZ))
            for j in range(ppd):
                index = 2 + dest * ppd + pick(j, ppd - 1 - j)

                def at(k, y):
                    return cur[pl.ds(pl.multiple_of(k * plane + row(y), nz), nz), cols]

                def emit(y, mid, total):
                    down, up = at(index + sign, y), at(index - sign, y)
                    cx = state(up, mid, down)
                    keep = pl.ds(y * nz, nz)
                    if j == 0:
                        before = state(at(index - 2 * sign, y), up, mid)
                    else:
                        before = cprev[keep]
                    if j < ppd - 1:
                        cprev[keep] = cx
                    result = mid - (total + rate_x * (cx - before))
                    sendbuf[index - 2, pl.ds(pl.multiple_of(row(y), nz), nz), cols] = result.astype(jnp.bfloat16)

                across(lambda y: at(index, y), emit, 0, hy)

    def own_lanes(v):
        return pl.ds(pl.multiple_of(v * width, width), width)

    def row_src(dest, h):
        return sendbuf.at[pl.ds(dest * ppd, ppd), pl.ds(pl.multiple_of(h * half, half), half)]

    def row_copy(dest, peer, r, h):
        return pltpu.make_async_remote_copy(
            src_ref=row_src(dest, h), dst_ref=recv.at[h, :, :, own_lanes(me)],
            send_sem=row_send.at[h, r], recv_sem=row_recv.at[h, r],
            device_id={"vel": peer}, device_id_type=MESH)

    def row_local(h):
        return pltpu.make_async_copy(row_src(mine, h), recv.at[h, :, :, own_lanes(me)], local_sem.at[0, h])

    def unit(dest, h):
        transport(dest, h)
        send(dest, h)

    def send(dest, h):
        peer = vel_of(slab, dest)
        r = lax.rem(peer - me + groups, groups)

        @pl.when(r == 0)
        def _():
            row_local(h).start()

        @pl.when(r != 0)
        def _():
            row_copy(dest, peer, r, h).start()

    def edge_dest(k):
        n = lax.rem(mine + k, 2 * edge)
        return n + lax.div(n, edge) * mid_count

    def near_dest(k):
        n = lax.rem(mine + k, 2 * edge)
        return edge + n + lax.div(n, edge) * far_count

    def far_dest(k):
        return 2 * edge + lax.rem(mine + k, far_count)

    def row_list(h):
        out = []
        for r in range(1, groups):
            peer = lax.rem(me + r, groups)
            out.append(row_copy(chain_of(slab, peer), peer, r, h))
        return out

    def z_copies(h):
        here = pl.ds(h * half, half)
        return [
            pltpu.make_async_remote_copy(
                src_ref=zsend.at[pl.ds(0, 2), here], dst_ref=zrecv.at[pl.ds(0, 2), here],
                send_sem=z_send.at[h, 0], recv_sem=z_recv.at[h, 0], device_id={"space": ahead}, device_id_type=MESH),
            pltpu.make_async_remote_copy(
                src_ref=zsend.at[pl.ds(2, 1), here], dst_ref=zrecv.at[pl.ds(2, 1), here],
                send_sem=z_send.at[h, 1], recv_sem=z_recv.at[h, 1], device_id={"space": behind}, device_id_type=MESH),
        ]

    def z_place(h):
        for copy in z_list[h]:
            copy.wait_recv()
        for n, at in enumerate((pick(0, nx + 2), pick(1, nx + 3), pick(nx + 2, 1))):
            here = pl.ds(pl.multiple_of(at * plane + h * half, half), half)
            cur[here] = zrecv[n, h * half:(h + 1) * half].astype(jnp.float32)

    def prepare():
        own = ppd * plane
        span = 4 * LANES
        base = mine * (own // LANES)
        eye = lax.broadcasted_iota(jnp.int32, (nz, nz), 0) == lax.broadcasted_iota(jnp.int32, (nz, nz), 1)
        columns = {}
        for j in range(ppd):
            sheet = relax[mine * ppd + j]
            for h in range(HALVES):
                parts = []
                for y in range(hy):
                    line = jnp.broadcast_to(sheet[h * hy + y:h * hy + y + 1, :], (nz, nz))
                    one = jnp.sum(jnp.where(eye, line, 0.0), axis=1, keepdims=True)
                    parts.append(jnp.broadcast_to(one, (nz, LANES)))
                columns[h, j] = jnp.concatenate(parts, axis=0)
        for step in range(STEPS):
            count = counts[step, slab]
            flags = jnp.zeros((16, LANES), jnp.float32)
            for n in range(cells // span):
                which = kin_cells[step:step + 1, n * span:(n + 1) * span]
                live = n * span + lax.broadcasted_iota(jnp.int32, (1, span), 1) < count
                quotient = jnp.where(live, lax.div(which, LANES) - base, -1)
                hot_high = lax.broadcasted_iota(jnp.int32, (16, span), 0) == quotient
                hot_low = lax.broadcasted_iota(jnp.int32, (LANES, span), 0) == lax.rem(which, LANES)
                flags += lax.dot_general(
                    jnp.where(hot_high, 1.0, 0.0).astype(jnp.bfloat16), jnp.where(hot_low, 1.0, 0.0).astype(jnp.bfloat16),
                    (((1,), (1,)), ((), ())), preferred_element_type=jnp.float32)
            for j in range(ppd):
                for h in range(HALVES):
                    n = j * HALVES + h
                    kin = jnp.broadcast_to(flags[n:n + 1], (LANES, LANES)).T > 0.5
                    rate = columns[h, j]
                    here = pl.ds(j * half, half)
                    coef[step, 0, h, here] = jnp.where(kin, 1.0, 1.0 - rate)
                    coef[step, 1, h, here] = jnp.where(kin, COLLIDE, rate)
                    coef[step, 2, h, here] = jnp.where(kin, 1.0, 0.0)

    def wide(x):
        return jnp.concatenate([x] * (TILE // LANES), axis=1)

    def collide(step, h):
        rows = recv.at[h]

        def lhs():
            return rows[...].reshape(block_rows, nv)

        @pl.loop(0, rank // TILE, unroll=True)
        def _(n):
            cols = pl.ds(pl.multiple_of(n * TILE, TILE), TILE)
            first = jnp.dot(lhs(), map_a[:, cols], preferred_element_type=jnp.float32)
            second = jnp.dot(lhs(), map_b[:, cols], preferred_element_type=jnp.float32)
            hid[:, cols] = (first * second * wide(coef[step, 2, h])).astype(jnp.bfloat16)

        mom = jnp.dot(lhs(), basis[...], preferred_element_type=jnp.float32)
        high = mom.astype(jnp.bfloat16).astype(jnp.float32)
        is_low = (lax.broadcasted_iota(jnp.int32, mom.shape, 1) // 8) == 1
        split = jnp.where(is_low, mom - high, high)
        hid[:, rank:rank + LANES] = (split * (1.0 - coef[step, 2, h])).astype(jnp.bfloat16)

        @pl.loop(0, nv // TILE)
        def _(n):
            cols = pl.ds(pl.multiple_of(n * TILE, TILE), TILE)
            out = jnp.dot(hid[...], map_c[:, cols], preferred_element_type=jnp.float32)
            for j in range(ppd):
                part = slice(j * half, (j + 1) * half)
                here = pl.ds(h * half, half)
                if step == 0:
                    old = rows[j, :, cols].astype(jnp.float32)
                else:
                    old = mv[j, here, cols]
                new = wide(coef[step, 0, h, part]) * old + wide(coef[step, 1, h, part]) * out[part]
                if step == 0:
                    fown[j, here, cols] = new
                    fsend[h, j, :, cols] = new.astype(jnp.bfloat16)
                else:
                    outbuf[h, j, :, cols] = new.astype(jnp.bfloat16)

    low, high_part = pl.ds(0, nv // 2), pl.ds(nv // 2, nv // 2)
    whole = pl.ds(0, nv)

    def halo_copies(h):
        out = []
        for k, (j, r, lanes) in enumerate((
                (reach * ppd - 2, reach, high_part), (ppd - 1, 1, whole), (0, -1, whole), (ppd + 1 - reach * ppd, -reach, low))):
            out.append(pltpu.make_async_remote_copy(
                src_ref=fsend.at[h, j, :, lanes], dst_ref=halo.at[h, k, :, lanes],
                send_sem=halo_send.at[h, k], recv_sem=halo_recv.at[h, k],
                device_id=along(r), device_id_type=MESH))
        return out

    def sideways(h, spans):
        @pl.loop(0, nv // LANES)
        def _(t):
            cols = pl.ds(pl.multiple_of(t * LANES, LANES), LANES)
            for j in range(ppd):
                def emit(y, mid, total):
                    mv[j, pl.ds((h * hy + y) * nz, nz), cols] = mid - total

                for first, last in spans:
                    across(lambda y: fown[j, pl.ds(((h * hy + y) % ny) * nz, nz), cols], emit, first, last)

    def forward(h):
        half_tiles = nv // LANES // 2
        for up in (-1, 1):
            @pl.loop(0, half_tiles)
            def _(n):
                t = n + (half_tiles if up > 0 else 0)
                cols = pl.ds(pl.multiple_of(t * LANES, LANES), LANES)
                rate_x = speed(t)

                def value(k, y):
                    here = pl.ds(y * nz, nz)
                    if 0 <= k < ppd:
                        return fown[k, pl.ds((h * hy + y) * nz, nz), cols]
                    slot = k + 2 if k < 0 else k - ppd + 2
                    return halo[h, slot, here, cols].astype(jnp.float32)

                order = list(range(ppd)) if up > 0 else list(range(ppd - 1, -1, -1))
                for y in range(hy):
                    line = [order[0] - 2 * up, order[0] - up] + order + [order[-1] + up]
                    f = [value(k, y) for k in line]
                    c = [state(f[n], f[n + 1], f[n + 2]) for n in range(ppd + 1)]
                    here = pl.ds((h * hy + y) * nz, nz)
                    for n, j in enumerate(order):
                        result = mv[j, here, cols] - rate_x * (c[n + 1] - c[n])
                        mv[j, here, cols] = result
                        recv[h, j, pl.ds(y * nz, nz), cols] = result.astype(jnp.bfloat16)

    def res_copies(h):
        out = []
        for r in range(1, groups):
            peer = lax.rem(me + r, groups)
            out.append(pltpu.make_async_remote_copy(
                src_ref=outbuf.at[h, :, :, own_lanes(peer)],
                dst_ref=ret_out.at[pl.ds(mine * ppd, ppd), pl.ds(h * half, half)],
                send_sem=res_send.at[h, r], recv_sem=res_recv.at[h, r],
                device_id={"vel": peer}, device_id_type=MESH))
        return out

    def res_local(h):
        return pltpu.make_async_copy(
            outbuf.at[h, :, :, own_lanes(me)],
            ret_out.at[pl.ds(mine * ppd, ppd), pl.ds(h * half, half)], local_sem.at[1, h])

    def widen(at, h):
        here = (pl.ds(at * ppd, ppd), pl.ds(h * half, half))
        wide_out[here] = ret_out[here].astype(jnp.float32)

    for copy in loads[:2 * edge + 1]:
        copy.wait()
    transport(mid_dest(0), 0)
    pl.semaphore_wait(barrier, groups + 1 + 2 * reach)
    send(mid_dest(0), 0)
    for copy in loads[2 * edge + 1:]:
        copy.wait()
    for n, at in enumerate((pick(nx, 2), pick(nx + 1, 3), pick(2, nx + 1))):
        zsend[n] = cur[pl.ds(pl.multiple_of(at * plane, plane), plane)].astype(jnp.bfloat16)
    z_list = [z_copies(h) for h in range(HALVES)]
    for copy in z_list[0] + z_list[1]:
        copy.start()
    for copy in consts:
        copy.start()

    @pl.loop(1, mid_count + 2 * edge)
    def _(k):
        h = lax.div(k, mid_count)
        unit((1 - h) * mid_dest(k) + h * near_dest(k), h)

    for copy in consts[5:]:
        copy.wait()
    prepare()
    z_place(0)

    @pl.loop(0, 2 * edge + far_count)
    def _(k):
        h = jnp.where(k < 2 * edge, 0, 1)
        unit((1 - h) * edge_dest(k) + h * far_dest(k), h)

    z_place(1)

    @pl.loop(0, 2 * edge)
    def _(k):
        unit(edge_dest(k), 1)

    for copy in consts[:5]:
        copy.wait()
    rows_in = [row_list(h) for h in range(HALVES)]
    halos = [halo_copies(h) for h in range(HALVES)]
    results = [res_copies(h) for h in range(HALVES)]
    inner, outer = [(2, hy - 2)], [(0, 2), (hy - 2, hy)]
    for h in range(HALVES):
        for copy in rows_in[h]:
            copy.wait_recv()
        row_local(h).wait()
        collide(0, h)
        for copy in halos[h]:
            copy.start()
        if h < HALVES - 1:
            sideways(h, inner)
    for h in range(HALVES):
        sideways(h, outer if h < HALVES - 1 else [(0, hy)])
        for copy in halos[h]:
            copy.wait_recv()
        forward(h)
        collide(1, h)
        for copy in results[h]:
            copy.start()
        res_local(h).start()
    for h in range(HALVES):
        for copy in z_list[h] + rows_in[h] + halos[h]:
            copy.wait_send()
        res_local(h).wait()
        widen(mine, h)
        for r, copy in enumerate(results[h], 1):
            copy.wait()
            widen(chain_of(slab, lax.rem(me - r + groups, groups)), h)


def body(dist, relax_rate, kinetic_cells, kinetic_count, map_a, map_b, map_c):
    nx, ny, nz, width = dist.shape
    groups = lax.axis_size("vel")
    slabs = lax.axis_size("space")
    cells = nx * ny * nz
    plane = ny * nz
    nv = groups * width
    rank = map_a.shape[1]
    ppd = nx // groups
    half = plane // HALVES
    basis, back = tables()

    any_space = pl.BlockSpec(memory_space=pl.ANY)
    f32, bf16 = jnp.float32, jnp.bfloat16
    dims = (nx, ny, nz, width, groups, slabs)
    vmem = pl.BlockSpec(memory_space=pltpu.VMEM)
    dma = pltpu.SemaphoreType.DMA
    ret = pl.pallas_call(
        functools.partial(kernel, dims),
        out_shape=pltpu.VMEM((nx, plane, width), f32),
        in_specs=[any_space] * 9,
        out_specs=vmem,
        scratch_shapes=[
            pltpu.VMEM(((nx + 4) * plane, width), f32),
            pltpu.VMEM((half, LANES), f32),
            pltpu.VMEM((nx, plane, width), bf16),
            pltpu.VMEM((3, plane, width), bf16),
            pltpu.VMEM((3, plane, width), bf16),
            pltpu.VMEM((HALVES, ppd, half, nv), bf16),
            pltpu.VMEM((ppd, plane, nv), f32),
            pltpu.VMEM((HALVES, ppd, half, nv), bf16),
            pltpu.VMEM((HALVES, 4, half, nv), bf16),
            pltpu.VMEM((ppd, plane, nv), f32),
            pltpu.VMEM((HALVES, ppd, half, nv), bf16),
            pltpu.VMEM(map_a.shape, bf16),
            pltpu.VMEM(map_b.shape, bf16),
            pltpu.VMEM((rank + LANES, nv), bf16),
            pltpu.VMEM((nv, LANES), bf16),
            pltpu.VMEM((ppd * half, rank + LANES), bf16),
            pltpu.VMEM((STEPS, 3, HALVES, ppd * half, LANES), f32),
            pltpu.SMEM(kinetic_count.shape, jnp.int32),
            pltpu.VMEM(kinetic_cells.shape, jnp.int32),
            pltpu.VMEM(relax_rate.shape, f32),
            pltpu.VMEM((nx, plane, width), bf16),
            dma((groups,)),
            dma((8,)),
            dma((2, HALVES)),
            dma((HALVES, 2)),
            dma((HALVES, 2)),
            dma((HALVES, groups)),
            dma((HALVES, groups)),
            dma((HALVES, 4)),
            dma((HALVES, 4)),
            dma((HALVES, groups)),
            dma((HALVES, groups)),
        ],
        compiler_params=pltpu.CompilerParams(
            collective_id=0, has_side_effects=True, vmem_limit_bytes=62783488),
    )(kinetic_count, kinetic_cells, relax_rate, dist.reshape(cells, width), map_a, map_b, map_c,
      jnp.asarray(basis), jnp.asarray(back))
    return ret.reshape(dist.shape)


def solution(mesh):
    return jax.shard_map(
        body,
        mesh=mesh,
        in_specs=(
            P("space", None, None, "vel"),
            P("space", None, None),
            P(None, "space"),
            P(),
            P(),
            P(),
            P(),
        ),
        out_specs=P("space", None, None, "vel"),
        check_vma=False,
    )
```
